256 devices in a mesh: mem: 64 (over x, z, core), rep: 4 (over y).
Axes of the slice: x: 4, y: 4, z: 8, core: 2. Of those that a mesh axis runs over, the one named last changes fastest.
Arguments:
- memory: float32 [65536, 172], P('mem'), may hold values from -6 to 6
- node_slot: int32 [65536], replicated, may hold values from 0 to 65535, as said below
- event_nodes: int32 [2, 32768, 33], P(None, ('mem', 'rep')), may hold values from 0 to 65535, as said below
- event_times: int32 [2, 32768], P(None, ('mem', 'rep')), may hold values from 0 to 999
- valid_mask: int32 [2, 32768], P(None, ('mem', 'rep')), may hold values 0 or 1
- time_freq: float32 [100], replicated, may hold values from 0.001 to 1
- time_phase: float32 [100], replicated, may hold values from -3.140625 to 3.140625
- gru_input: bfloat16 [444, 516], replicated, may hold values from -0.25 to 0.25
- gru_hidden: bfloat16 [172, 516], replicated, may hold values from -0.4375 to 0.4375
- gru_in_bias: float32 [516], replicated, may hold values from -3 to 3
- gru_hid_bias: float32 [516], replicated, may hold values from -3 to 3
- w_self: float32 [172, 100], replicated, may hold values from -0.4375 to 0.4375
- w_nbr: float32 [172, 100], replicated, may hold values from -0.4375 to 0.4375
- b_embed: float32 [100], replicated, may hold values from -3 to 3
- w_dec1: float32 [200, 100], replicated, may hold values from -0.4375 to 0.4375
- b_dec1: float32 [100], replicated, may hold values from -3 to 3
- w_dec2: float32 [100], replicated, may hold values from -0.625 to 0.625
- b_dec2: float32 [1], replicated, may hold values from -3 to 3
Outputs:
- memory_out: float32 [65536, 172], P('mem')
- batch_losses: float32 [2], replicated
- w_self_out: float32 [172, 100], replicated
- w_nbr_out: float32 [172, 100], replicated
- b_embed_out: float32 [100], replicated
- w_dec1_out: float32 [200, 100], replicated
- b_dec1_out: float32 [100], replicated
- w_dec2_out: float32 [100], replicated
- b_dec2_out: float32 [1], replicated
The draws below stay inside these ranges and needn't reach their ends.
Inputs may be any that keep to these rules, and one draw needn't show every extreme that they name: A permutation: node n's memory is row node_slot[n] of memory. `event_nodes`: columns 0, 1, 2 of an event are its source, destination and negative node; column 3 + r * 10 + k is neighbour k of column r. Among one device's events of one batch, the nodes of columns 0 and 1 whose slots lie in one block of 1024 slots are at most 8, and those of the other columns at most 78; in every such group of events one block of slots receives exactly 8 and 78.
All inputs are finite; a program needn't handle non-finite values. No bound on the sum of `valid_mask` on one device may be relied on, other than what follows from the above.
Results may differ from the reference program's by a relative error of at most 0.002.
Values may be sent and summed in bfloat16 or wider, within the bound.
No kernel may reach another device: no remote copies, remote signals or barrier semaphores. Data moves between devices by JAX's collectives and lax.ppermute only.
A program may use at most 128 MiB of HBM per device.

```python
import math
import jax
import jax.numpy as jnp
from jax import lax

DM = 172
DE = 100
DT = 100
K = 10
BATCHES = 2
NODE_DEV = 1024
EV_DEV = 128
MSGW = 444
NODES = 65536
EVENTS = 32768
CAP2 = 8
CAP_R = 78


def slot_table(key):
    return jax.random.permutation(jax.random.fold_in(key, 11), NODES).astype(jnp.int32)


def owner_pick(key, how_many, bound, owners, favored):
    total = owners * bound
    owner_pool = jnp.arange(total, dtype=jnp.int32) % owners
    scores = jax.random.permutation(key, total).astype(jnp.int32)
    scores = jnp.where(owner_pool == favored, scores - total, scores)
    ranking = jnp.argsort(scores, stable=True)
    chosen = owner_pool[ranking[:how_many]]
    return jax.random.permutation(jax.random.fold_in(key, 3), chosen)


def event_block(key, inverse):
    owners = NODES // NODE_DEV
    favored = jax.random.randint(jax.random.fold_in(key, 1), (), 0, owners).astype(jnp.int32)
    paired = owner_pick(jax.random.fold_in(key, 2), 2 * EV_DEV, CAP2, owners, favored)
    others = owner_pick(jax.random.fold_in(key, 4), (3 * K + 1) * EV_DEV, CAP_R, owners, favored)
    holder = jnp.concatenate([paired.reshape(EV_DEV, 2), others.reshape(EV_DEV, 3 * K + 1)], 1)
    offsets = jax.random.randint(jax.random.fold_in(key, 5), (EV_DEV, 3 * K + 3), 0, NODE_DEV).astype(jnp.int32)
    return inverse[holder * NODE_DEV + offsets]


def draw_node_slot(key, part):
    return slot_table(key)


def draw_event_nodes(key, part):
    inverse = jnp.argsort(slot_table(key)).astype(jnp.int32)
    blocks = BATCHES * (EVENTS // EV_DEV)
    keys = jax.random.split(jax.random.fold_in(key, 12), blocks)
    result = jax.vmap(lambda block_key: event_block(block_key, inverse))(keys)
    return result.reshape(BATCHES, EVENTS, 3 * K + 3).astype(jnp.int32)


def place_ends(drawn, stream_key, smallest, top_value):
    index_at = [jax.random.randint(jax.random.fold_in(stream_key, axis), (), 0, length) for axis, length in enumerate(drawn.shape)]
    main_axis = drawn.shape.index(max(drawn.shape))
    next_to = index_at[:main_axis] + [(index_at[main_axis] + 1) % drawn.shape[main_axis]] + index_at[main_axis + 1:]
    return drawn.at[tuple(index_at)].set(smallest).at[tuple(next_to)].set(top_value)


def block_levels(own_key, extent, cuts, least, top_value):
    level = 1.0
    for axis_at, blocks in cuts:
        heights = jax.random.uniform(jax.random.fold_in(jax.random.fold_in(own_key, 6), axis_at), (blocks,), jnp.float32, least / len(cuts), top_value / len(cuts))
        level = level * jnp.repeat(jnp.exp(heights), extent[axis_at] // blocks).reshape((-1,) + (1,) * (len(extent) - 1 - axis_at))
    return level


def noise(stream_key, dims, width, limit, shards=(), held_as=jnp.bfloat16):
    level = block_levels(stream_key, dims, shards, -0.22, 0.18) if shards else 1.0
    values = jax.random.normal(stream_key, dims, jnp.float32) * width * level
    return jnp.minimum(jnp.maximum(values, -limit), limit).astype(held_as)


def setup_inputs(seed: int = 0) -> dict:
    seeds = jax.random.split(jax.random.key(seed), 19)
    return {
        "memory": noise(seeds[0], (NODES, DM), 1.0, 6.0, ((0, 64),), jnp.float32),
        "node_slot": draw_node_slot(jax.random.fold_in(seeds[18], 71), 0),
        "event_nodes": draw_event_nodes(jax.random.fold_in(seeds[18], 71), 0),
        "event_times": place_ends(jax.random.randint(seeds[3], (BATCHES, EVENTS), 0, 1000), jax.random.fold_in(seeds[3], 1), 0, 999).astype(jnp.int32),
        "valid_mask": place_ends((jax.random.randint(seeds[4], (BATCHES, EVENTS), 0, 4) < 3).astype(jnp.int32), jax.random.fold_in(seeds[4], 1), 0, 1),
        "time_freq": jnp.clip(jnp.exp(jax.random.uniform(seeds[5], (DT,), jnp.float32, math.log(0.001), math.log(1.0))), 0.001, 1.0),
        "time_phase": jnp.clip(jax.random.uniform(seeds[6], (DT,), jnp.float32, -3.140625, 3.140625), -3.140625, 3.140625),
        "gru_input": noise(seeds[7], (MSGW, 3 * DM), MSGW ** -0.5, 0.25),
        "gru_hidden": noise(seeds[8], (DM, 3 * DM), DM ** -0.5, 0.4375),
        "gru_in_bias": noise(seeds[9], (3 * DM,), 0.5, 3.0, (), jnp.float32),
        "gru_hid_bias": noise(seeds[10], (3 * DM,), 0.5, 3.0, (), jnp.float32),
        "w_self": noise(seeds[11], (DM, DE), DM ** -0.5, 0.4375, (), jnp.float32),
        "w_nbr": noise(seeds[12], (DM, DE), DM ** -0.5, 0.4375, (), jnp.float32),
        "b_embed": noise(seeds[13], (DE,), 0.5, 3.0, (), jnp.float32),
        "w_dec1": noise(seeds[14], (2 * DE, DE), (2 * DE) ** -0.5, 0.4375, (), jnp.float32),
        "b_dec1": noise(seeds[15], (DE,), 0.5, 3.0, (), jnp.float32),
        "w_dec2": noise(seeds[16], (DE,), DE ** -0.5, 0.625, (), jnp.float32),
        "b_dec2": noise(seeds[17], (1,), 0.5, 3.0, (), jnp.float32),
    }


step_size = 4.0

def block_loss(current, fetched, valid_part):
    w_self, w_nbr, b_embed, w_dec1, b_dec1, w_dec2, b_dec2 = current
    num_events = fetched.shape[0]
    row_width = fetched.shape[2]
    neighbours = (fetched.shape[1] - 3) // 3
    embed_width = w_self.shape[1]
    own_rows = fetched[:, :3].reshape(num_events * 3, row_width)
    beside_all = fetched[:, 3:].reshape(num_events * 3 * neighbours, row_width)
    direct = jnp.dot(own_rows, w_self.astype(jnp.bfloat16), preferred_element_type=jnp.float32).reshape(num_events, 3, embed_width)
    spread = jnp.dot(beside_all, w_nbr.astype(jnp.bfloat16), preferred_element_type=jnp.float32).reshape(num_events, 3, neighbours, embed_width)
    hidden = jnp.tanh(direct + lax.optimization_barrier(jnp.mean(spread, 2)) + b_embed).astype(jnp.bfloat16)
    paired = jnp.concatenate([jnp.concatenate([hidden[:, 0], hidden[:, 1]], 1), jnp.concatenate([hidden[:, 0], hidden[:, 2]], 1)], 0)
    inner_act = jax.nn.relu(jnp.dot(paired, w_dec1.astype(jnp.bfloat16), preferred_element_type=jnp.float32) + b_dec1)
    logits = lax.optimization_barrier(jnp.sum(inner_act * w_dec2, 1)) + b_dec2[0]
    weights = valid_part.astype(jnp.float32)
    sign_flip = jnp.concatenate([-jnp.ones((num_events,), jnp.float32), jnp.ones((num_events,), jnp.float32)])
    return jnp.sum(jax.nn.softplus(sign_flip * logits) * jnp.concatenate([weights, weights]))

def normalized_step(params, gradients):
    total = jnp.zeros((), jnp.float32)
    for grad_part in gradients:
        total = total + jnp.sum(grad_part * grad_part)
    factor = step_size / (jnp.sqrt(total) + 1e-06)
    return tuple((value - factor * grad_part for value, grad_part in zip(params, gradients)))

def memory_update(mean_bf, state_bf, old_state, gru_input, gru_hidden, gru_in_bias, gru_hid_bias):
    row_width = old_state.shape[1]
    from_input = jnp.dot(mean_bf, gru_input, preferred_element_type=jnp.float32) + gru_in_bias
    from_state = jnp.dot(state_bf, gru_hidden, preferred_element_type=jnp.float32) + gru_hid_bias
    reset = jax.nn.sigmoid(from_input[:, :row_width] + from_state[:, :row_width])
    update = jax.nn.sigmoid(from_input[:, row_width:2 * row_width] + from_state[:, row_width:2 * row_width])
    candidate = jnp.tanh(from_input[:, 2 * row_width:] + reset * from_state[:, 2 * row_width:])
    return (1.0 - update) * candidate + update * old_state

def reference(memory, node_slot, event_nodes, event_times, valid_mask, time_freq, time_phase, gru_input, gru_hidden, gru_in_bias, gru_hid_bias, w_self, w_nbr, b_embed, w_dec1, b_dec1, w_dec2, b_dec2):
    params = (w_self, w_nbr, b_embed, w_dec1, b_dec1, w_dec2, b_dec2)
    losses = []
    blocks = EVENTS // EV_DEV
    columns = 3 * K + 3
    for batch_index in range(BATCHES):
        slot_ids = node_slot[event_nodes[batch_index]]
        memory_bf = memory.astype(jnp.bfloat16)

        def one_block(pieces):
            block_slots, block_valid = pieces
            fetched = memory_bf[block_slots]
            loss_part, pullback = jax.vjp(lambda current: block_loss(current, fetched, block_valid), params)
            return (loss_part, pullback(jnp.ones_like(loss_part))[0])
        loss_parts, grad_parts = lax.map(one_block, (slot_ids.reshape(blocks, EV_DEV, columns), valid_mask[batch_index].reshape(blocks, EV_DEV)))
        gradients = tuple((lax.optimization_barrier(jnp.sum(grad_part, 0)) for grad_part in grad_parts))
        loss_total = jnp.sum(loss_parts)
        count_total = jnp.sum(valid_mask[batch_index].astype(jnp.float32))
        losses.append(loss_total / jnp.maximum(count_total, 1.0))
        params = normalized_step(params, gradients)
        time_code = jnp.cos(event_times[batch_index].astype(jnp.float32)[:, None] * time_freq + time_phase).astype(jnp.bfloat16)
        source = memory_bf[slot_ids[:, 0]]
        target_rows = memory_bf[slot_ids[:, 1]]
        letters = jnp.stack([jnp.concatenate([source, target_rows, time_code], 1), jnp.concatenate([target_rows, source, time_code], 1)], 1).reshape(2 * EVENTS, -1)
        aims = slot_ids[:, :2].reshape(-1)
        summed = jax.ops.segment_sum(letters.astype(jnp.float32), aims, num_segments=NODES)
        counts = jax.ops.segment_sum(jnp.ones((2 * EVENTS,), jnp.float32), aims, num_segments=NODES)
        mean_bf = (summed / jnp.maximum(counts, 1.0)[:, None]).astype(jnp.bfloat16)
        fresh = memory_update(mean_bf, memory_bf, memory, gru_input, gru_hidden, gru_in_bias, gru_hid_bias)
        memory = jnp.where(counts[:, None] > 0, fresh, memory)
    return (memory, jnp.stack(losses), params[0], params[1], params[2], params[3], params[4], params[5], params[6])
```

```python
import functools

import jax
import jax.numpy as jnp
from jax import lax
from jax.experimental import pallas as pl
from jax.experimental.pallas import tpu as pltpu
from jax.sharding import Mesh
from jax.sharding import PartitionSpec as P

HOME = ("x", "zh", "zl", "c")
SLAB = ("x", "y", "zl", "c")
ALL = ("x", "zh", "zl", "c", "y")
ZH = 4
OWNERS = 64
EVENTS = 128
WIDTH = 172
EMBED = 100
SLOTS = 1024
PAIR = 8 * ZH
ROWS = 112
HALF = 56
LEFT = WIDTH - 128
POSITIONS = OWNERS * ROWS
CHUNK = 16
STEP = 4.0
F32 = jnp.float32
BF = jnp.bfloat16
I32 = jnp.int32
AT_NBR, AT_DEC_A, AT_DEC_B, AT_VEC = 176, 352, 456, 560
PARAM_ROWS = 568
GRAD_ROWS = OWNERS * CHUNK


def iota(shape, dim):
    return lax.broadcasted_iota(I32, shape, dim)


def mm(a, b):
    return jnp.dot(a, b, preferred_element_type=F32)


def mm_nt(a, b):
    return lax.dot_general(a, b, (((1,), (1,)), ((), ())), preferred_element_type=F32)


def call(kernel, out_shape, *args, flops=1e8, **kw):
    moved = sum(a.size * a.dtype.itemsize for a in args)
    return pl.pallas_call(
        kernel,
        out_shape=out_shape,
        compiler_params=pltpu.CompilerParams(vmem_limit_bytes=56 << 20),
        cost_estimate=pl.CostEstimate(flops=int(flops), bytes_accessed=int(moved), transcendentals=0),
        **kw,
    )(*args)


def sds(shape, dtype):
    return jax.ShapeDtypeStruct(shape, dtype)


def route_kernel(ids_ref, table_ref, req_ref, group_ref, place_ref, slot_ref, table_t):
    t = table_ref[...]
    table_t[0:128, :] = jnp.transpose((t >> 8).astype(F32)).astype(BF)
    table_t[128:256, :] = jnp.transpose((t & 255).astype(F32)).astype(BF)
    upper = (iota((128, 128), 0) < iota((128, 128), 1)).astype(F32)
    both = jnp.concatenate([upper, jnp.ones((128, 128), F32)], 1).astype(BF)
    lane = iota((1, 128), 1)
    acc = jnp.zeros((4 * OWNERS, 128), F32)
    base = jnp.zeros((OWNERS, 128), F32)
    for part in range(5):
        ids = [ids_ref[part * 8 + r : part * 8 + r + 1, :] for r in range(8)]
        rows = 7 if part == 4 else 8
        hot = jnp.concatenate(
            [(iota((512, 128), 0) == (n >> 7)).astype(F32).astype(BF) for n in ids[:rows]], 1
        )
        picked = mm(table_t[...], hot)
        sent = []
        slots = []
        for r in range(rows):
            low = iota((128, 128), 0) == (ids[r] & 127)
            hi = jnp.sum(jnp.where(low, picked[:128, r * 128 : (r + 1) * 128], 0.0), 0, keepdims=True)
            lo = jnp.sum(jnp.where(low, picked[128:, r * 128 : (r + 1) * 128], 0.0), 0, keepdims=True)
            slot = (hi * 256.0 + lo).astype(I32)
            slots.append(slot & (SLOTS - 1))
            sent.append(slot >> 10)
        own = [iota((OWNERS, 128), 0) == d for d in sent]
        own_f = [o.astype(F32) for o in own]
        counted = mm(jnp.concatenate([o.astype(BF) for o in own_f], 0), both)
        for r in range(rows):
            mine = counted[r * OWNERS : (r + 1) * OWNERS]
            if part == 0 and r % 2 == 0:
                base = jnp.zeros((OWNERS, 128), F32)
            if part == 1 and r == 0:
                base = jnp.zeros((OWNERS, 128), F32)
            rank = jnp.sum(own_f[r] * (mine[:, :128] + base), 0, keepdims=True).astype(I32)
            base = base + mine[:, 128:]
            plus = slots[r] + 1
            if part == 0:
                where = (r // 2) * 8 + rank
                place_ref[r : r + 1, :] = sent[r] * 8 + rank
                slot_ref[r : r + 1, :] = plus
                ghi = glo = jnp.zeros((1, 128), F32)
            else:
                where = PAIR + rank
                row = (part - 1) * 8 + r
                kind = 3 if row == 0 else (row - 1) // 10
                ghi = jnp.full((1, 128), float(kind + 1), F32)
                glo = lane.astype(F32)
            at = (iota((128, 128), 0) == where).astype(F32).astype(BF)
            planes = [(slots[r] >> 5).astype(F32) + 1.0, (slots[r] & 31).astype(F32), ghi, glo]
            left = jnp.concatenate([own_f[r] * v for v in planes], 0).astype(BF)
            acc = acc + mm_nt(left, at)
    o = OWNERS
    req_ref[...] = ((acc[0:o] - 1.0) * 32.0 + acc[o : 2 * o]).astype(I32)
    group_ref[...] = ((acc[2 * o : 3 * o] - 1.0) * 128.0 + acc[3 * o :]).astype(I32)


def route(ids, table):
    return call(
        route_kernel,
        (sds((OWNERS, 128), I32), sds((OWNERS, 128), I32), sds((8, 128), I32), sds((8, 128), I32)),
        ids,
        table,
        flops=3e9,
        scratch_shapes=[pltpu.VMEM((256, 512), BF)],
    )


def gather_kernel(want_ref, mem_ref, extra_ref, out_ref, mem_rows, *, shared):
    @pl.when(pl.program_id(0) == 0)
    def _():
        m = jnp.concatenate([mem_ref[...], jnp.zeros((4, SLOTS), F32)], 0)
        mem_rows[:, 0:128] = jnp.transpose(m[0:128]).astype(BF)
        tail = jnp.concatenate([m[128:], jnp.zeros((80, SLOTS), F32)], 0)
        mem_rows[:, 128:256] = jnp.transpose(tail).astype(BF)

    cols = jnp.transpose(want_ref[...].astype(F32)).astype(I32)
    lane = iota((ROWS, SLOTS), 1)
    hot = jnp.concatenate(
        [(lane == cols[0:ROWS, j : j + 1]).astype(F32).astype(BF) for j in range(8)], 0
    )
    rows = mm(hot, mem_rows[...])
    for j in range(8):
        mine = rows[j * ROWS : (j + 1) * ROWS]
        tail = mine[:HALF, 128:] + pltpu.roll(mine[HALF:, 128:], 64, 1)
        extra = extra_ref[...] if shared else extra_ref[j]
        out_ref[j, 0:ROWS, :] = mine[:, :128].astype(BF)
        out_ref[j, ROWS : ROWS + HALF, :] = tail.astype(BF)
        out_ref[j, ROWS + HALF :, :] = extra


def gather(want, mem_t, extra, shared):
    more = extra.shape[-2]
    total = ROWS + HALF + more
    if shared:
        extra_spec = pl.BlockSpec((more, 128), lambda i: (0, 0))
    else:
        extra_spec = pl.BlockSpec((8, more, 128), lambda i: (i, 0, 0))
    return call(
        functools.partial(gather_kernel, shared=shared),
        sds((OWNERS, total, 128), BF),
        want,
        mem_t,
        extra,
        flops=4e9,
        grid=(8,),
        in_specs=[
            pl.BlockSpec((8, 128), lambda i: (i, 0)),
            pl.BlockSpec((WIDTH, SLOTS), lambda i: (0, 0)),
            extra_spec,
        ],
        out_specs=pl.BlockSpec((8, total, 128), lambda i: (i, 0, 0)),
        scratch_shapes=[pltpu.VMEM((SLOTS, 256), BF)],
    )


def stepped(params, grads):
    row, col = iota((PARAM_ROWS, 128), 0), iota((PARAM_ROWS, 128), 1)
    real = (row < AT_VEC + 3) | ((row == AT_VEC + 3) & (col == 0))
    grads = jnp.where(real, grads, 0.0)
    norm = jnp.sqrt(jnp.sum(grads * grads))
    return params - (STEP / (norm + 1e-06)) * grads


def vectors_of(grads):
    return grads[AT_VEC : AT_VEC + 8] + grads[AT_VEC + 8 : AT_VEC + 16] + grads[AT_VEC + 16 : AT_VEC + 24]


def joined(flat):
    return jnp.concatenate([flat[:AT_VEC], vectors_of(flat)], 0)


def softplus(x):
    return jnp.maximum(x, 0.0) + jnp.log1p(jnp.exp(-jnp.abs(x)))


def loss_kernel(*refs, update):
    (rows_ref, group_ref, place_ref, slot_ref, time_ref, zh_ref, valid_ref, param_ref), outs = refs[:8], refs[8:]
    if update:
        out_ref, param_out_ref, prev_ref, rows256, select = outs
        got = rows_ref[:, ROWS + HALF :, :].astype(F32)
        flat = (got[:, :CHUNK] + got[:, CHUNK:]).reshape(GRAD_ROWS, 128)
        grads = joined(flat)
        params = stepped(param_ref[...], grads)
        param_out_ref[...] = params
        prev_ref[...] = grads[AT_VEC:]
    else:
        out_ref, rows256, select = outs
        params = param_ref[...]

    rows256[:, :, 0:128] = rows_ref[:, 0:ROWS, :]
    tails = rows_ref[:, ROWS : ROWS + HALF, :]
    rows256[:, 0:HALF, 128:256] = tails
    rows256[:, HALF:ROWS, 128:256] = pltpu.roll(tails.astype(F32), 64, 2).astype(BF)

    for t in range(POSITIONS // 128):
        select[:, t * 128 : (t + 1) * 128] = (
            iota((512, 128), 0) == group_ref[t : t + 1, :]
        ).astype(F32).astype(BF)
    summed = mm(select[...], rows256[...].reshape(POSITIONS, 256))
    nbr = summed[: 3 * EVENTS]

    lane256 = iota((EVENTS, 256), 1)
    place = place_ref[...]
    place_c = jnp.transpose(place.astype(F32)).astype(I32)
    plus = slot_ref[...]
    time = time_ref[...]
    info = jnp.concatenate(
        [(plus >> 5).astype(F32), (plus & 31).astype(F32), (time >> 5).astype(F32), (time & 31).astype(F32)], 0
    )
    info_c = jnp.transpose(info)

    tails_out = []
    own = []
    for d in range(ZH):
        held = rows256[:, d * 8 : (d + 1) * 8, :].reshape(OWNERS * 8, 256)
        picked = []
        spread = []
        marked = []
        for c in range(2):
            r = 2 * d + c
            take = (iota((EVENTS, OWNERS * 8), 1) == place_c[:, r : r + 1]).astype(F32).astype(BF)
            x = mm(take, held)
            picked.append(jnp.where(lane256 < WIDTH, x, 0.0))
            spread.append((iota((OWNERS * 8, EVENTS), 0) == place[r : r + 1, :]).astype(F32).astype(BF))
            marks = jnp.zeros((EVENTS, 256), F32)
            for k, col in enumerate((r, 8 + r, 16 + d, 20 + d)):
                marks = jnp.where(lane256 == WIDTH + k, info_c[:, col : col + 1], marks)
            marked.append(marks)
        to_first = (picked[1] + marked[0]).astype(BF)
        to_second = (picked[0] + marked[1]).astype(BF)
        letters = mm(spread[0], to_first) + mm(spread[1], to_second)
        out_ref[:, d * 8 : (d + 1) * 8, :] = letters[:, :128].reshape(OWNERS, 8, 128).astype(BF)
        tails_out.append(letters[:, 128:])
        mine = (zh_ref[...] == d).astype(F32)
        own = [p * mine if d == 0 else o + p * mine for p, o in zip(picked, own or picked)]
    for d in range(2):
        tail = tails_out[d] + pltpu.roll(tails_out[d + 2], 64, 1)
        out_ref[:, PAIR + d * 8 : PAIR + (d + 1) * 8, :] = tail.reshape(OWNERS, 8, 128).astype(BF)

    own_rows = jnp.concatenate(own + [jnp.where(lane256 < WIDTH, summed[3 * EVENTS :], 0.0)], 0).astype(BF)
    zeros = jnp.zeros((80, 128), F32)
    w_self = jnp.concatenate([params[0:AT_NBR], zeros], 0).astype(BF)
    w_nbr = jnp.concatenate([params[AT_NBR:AT_DEC_A], zeros], 0).astype(BF)
    pad = jnp.zeros((24, 128), F32)
    dec_a = jnp.concatenate([params[AT_DEC_A:AT_DEC_B], pad], 0).astype(BF)
    dec_b = jnp.concatenate([params[AT_DEC_B:AT_VEC], pad], 0).astype(BF)
    b_embed = params[AT_VEC : AT_VEC + 1]
    b_dec1 = params[AT_VEC + 1 : AT_VEC + 2]
    w_dec2 = params[AT_VEC + 2 : AT_VEC + 3]
    b_dec2 = params[AT_VEC + 3 : AT_VEC + 4, 0:1]
    nbr_hi = nbr.astype(BF)
    nbr_lo = (nbr - nbr_hi.astype(F32)).astype(BF)
    mean = (mm(nbr_hi, w_nbr) + mm(nbr_lo, w_nbr)) * 0.1
    act = jnp.tanh(mm(own_rows, w_self) + mean + b_embed)
    hidden = act.astype(BF)
    first = jnp.concatenate([hidden[:EVENTS], hidden[:EVENTS]], 0)
    second = hidden[EVENTS:]
    pre = mm(first, dec_a) + mm(second, dec_b) + b_dec1
    inner = jnp.maximum(pre, 0.0)
    logits = jnp.sum(inner * w_dec2, 1, keepdims=True) + b_dec2
    valid_row = valid_ref[...].astype(F32)
    valid = jnp.transpose(jnp.broadcast_to(valid_row, (128, 128)))[:, 0:1]
    valid = jnp.concatenate([valid, valid], 0)
    sign = jnp.where(iota((2 * EVENTS, 1), 0) < EVENTS, -1.0, 1.0)
    loss = jnp.sum(softplus(sign * logits) * valid)
    count = jnp.sum(valid_row)
    d_logit = sign * jax.nn.sigmoid(sign * logits) * valid
    d_inner = jnp.where(pre > 0.0, d_logit * w_dec2, 0.0)
    d_bf = d_inner.astype(BF)
    g_dec2 = jnp.sum(inner * d_logit, 0, keepdims=True)
    g_b2 = jnp.sum(d_logit)
    g_b1 = jnp.sum(d_inner, 0, keepdims=True)
    d_first = mm_nt(d_bf, dec_a).astype(BF).astype(F32)
    d_second = mm_nt(d_bf, dec_b).astype(BF).astype(F32)
    d_zero = (d_first[:EVENTS] + d_first[EVENTS:]).astype(BF).astype(F32)
    d_pre = jnp.concatenate([d_zero, d_second], 0) * (1.0 - act * act)
    g_be = jnp.sum(d_pre, 0, keepdims=True)

    def mm_tn(a, b):
        return mm(jnp.transpose(a.astype(F32)).astype(BF), b)

    g_self = mm_tn(own_rows, d_pre.astype(BF))[:176]
    d_mean = (d_pre * 0.1).astype(BF)
    g_nbr = (mm_tn(nbr_hi, d_mean) + mm_tn(nbr_lo, d_mean))[:176]
    g_nbr = jnp.where(iota((176, 128), 0) < WIDTH, g_nbr, 0.0)
    g_a = mm_tn(first, d_bf)[:104]
    g_b = mm_tn(second, d_bf)[:104]
    one = jnp.ones((1, 128), F32)
    vec = jnp.concatenate([g_be, g_b1, g_dec2, g_b2 * one, loss * one, count * one, one * 0.0, one * 0.0], 0)
    hi = vec.astype(BF).astype(F32)
    mid = (vec - hi).astype(BF).astype(F32)
    low = vec - hi - mid
    rest = jnp.zeros((GRAD_ROWS - AT_VEC - 24, 128), F32)
    grads = jnp.concatenate([g_self, g_nbr, g_a, g_b, hi, mid, low, rest], 0)
    out_ref[:, PAIR + CHUNK :, :] = grads.reshape(OWNERS, CHUNK, 128).astype(BF)


def loss_and_letters(rows, group, place, slot, time, zh, valid, params, update):
    out = [sds((OWNERS, PAIR + CHUNK + CHUNK, 128), BF)]
    if update:
        out += [sds((PARAM_ROWS, 128), F32), sds((8, 128), F32)]
    return call(
        functools.partial(loss_kernel, update=update),
        tuple(out),
        rows,
        group,
        place,
        slot,
        time,
        zh,
        valid,
        params,
        flops=1e10,
        scratch_shapes=[pltpu.VMEM((OWNERS, ROWS, 256), BF), pltpu.VMEM((512, POSITIONS), BF)],
    )


def final_kernel(got_ref, param_ref, prev_ref, loss_ref, ws_ref, wn_ref, be_ref, wd_ref, b1_ref, w2_ref, b2_ref):
    grads = joined(got_ref[...].reshape(GRAD_ROWS, 128))
    params = stepped(param_ref[...], grads)
    vec = grads[AT_VEC:]
    prev = prev_ref[...]
    first = prev[4:5] / jnp.maximum(prev[5:6], 1.0)
    second = vec[4:5] / jnp.maximum(vec[5:6], 1.0)
    loss_ref[...] = jnp.where(iota((1, 128), 1) == 0, first, second)[:, 0:2]
    ws_ref[...] = params[0:WIDTH, :EMBED]
    wn_ref[...] = params[AT_NBR : AT_NBR + WIDTH, :EMBED]
    wd_ref[0:EMBED, :] = params[AT_DEC_A : AT_DEC_A + EMBED, :EMBED]
    wd_ref[EMBED:, :] = params[AT_DEC_B : AT_DEC_B + EMBED, :EMBED]
    be_ref[...] = params[AT_VEC : AT_VEC + 1, :EMBED]
    b1_ref[...] = params[AT_VEC + 1 : AT_VEC + 2, :EMBED]
    w2_ref[...] = params[AT_VEC + 2 : AT_VEC + 3, :EMBED]
    b2_ref[...] = params[AT_VEC + 3 : AT_VEC + 4, 0:1]


def gru_kernel(
    got_ref, mem_ref, seen_ref, freq_ref, phase_ref, w_in_ref, w_st_ref, b_in_ref, b_st_ref, *outs, last
):
    hot, stack = outs[-2:]
    half = PAIR // 2
    for h in range(2):
        n = OWNERS * half
        head = got_ref[:, h * half : (h + 1) * half, :].reshape(n, 128).astype(F32)
        tail = got_ref[:, PAIR : PAIR + half, :].reshape(n, 128).astype(F32)
        if h:
            tail = pltpu.roll(tail, 64, 1)
        col = (tail[:, LEFT : LEFT + 1] * 32.0 + tail[:, LEFT + 1 : LEFT + 2]).astype(I32) - 1
        hot[h * n : (h + 1) * n, :] = (iota((n, SLOTS), 1) == col).astype(F32).astype(BF)
        here = pl.ds(h * n, n)
        tail_t = jnp.transpose(tail)[0:48]
        when = tail_t[46:47] * 32.0 + tail_t[47:48]
        code = jnp.cos(freq_ref[...] * when + phase_ref[...])
        stack[0:128, here] = jnp.transpose(head).astype(BF)
        stack[128:176, here] = jnp.where(iota((48, n), 0) == LEFT, 1.0, tail_t).astype(BF)
        stack[176:280, here] = code.astype(BF)
    summed = mm(stack[...], hot[...])
    counts = summed[WIDTH : WIDTH + 1]
    mean = (summed / jnp.maximum(counts, 1.0)).astype(BF)
    mem = mem_ref[...]
    mem_pad = jnp.concatenate([mem, jnp.zeros((4, SLOTS), F32)], 0)
    state = mem_pad.astype(BF)
    from_in = mm(w_in_ref[...], jnp.concatenate([state, mean], 0)) + b_in_ref[...]
    from_st = mm(w_st_ref[...], state) + b_st_ref[...]
    reset = jax.nn.sigmoid(from_in[0:176] + from_st[0:176])
    update = jax.nn.sigmoid(from_in[176:352] + from_st[176:352])
    candidate = jnp.tanh(from_in[352:528] + reset * from_st[352:528])
    fresh = (1.0 - update) * candidate + update * mem_pad
    new = jnp.where(counts > 0.0, fresh, mem_pad)
    seen = jnp.maximum(counts, seen_ref[...])
    if last:
        flag = jnp.minimum(seen, 1.0)
        outs[0][...] = jnp.where(iota((176, SLOTS), 0) == WIDTH, flag, new).astype(BF)
    else:
        outs[0][...] = new[:WIDTH]
        outs[1][...] = seen


def gru(got, mem_t, seen, weights, last):
    n = OWNERS * PAIR
    if last:
        out = (sds((176, SLOTS), BF),)
    else:
        out = (sds((WIDTH, SLOTS), F32), sds((1, SLOTS), F32))
    return call(
        functools.partial(gru_kernel, last=last),
        out,
        got,
        mem_t,
        seen,
        *weights,
        flops=3e9,
        scratch_shapes=[pltpu.VMEM((n, SLOTS), BF), pltpu.VMEM((280, n), BF)],
    )


def gru_weights(gru_input, gru_hidden, gru_in_bias, gru_hid_bias, time_freq, time_phase):
    def rows(a, to):
        return jnp.pad(a, [(0, 0), (0, to - a.shape[1])] + [(0, 0)] * (a.ndim - 2))

    w_in = gru_input.T.reshape(3, WIDTH, -1)
    parts = [w_in[:, :, :WIDTH], w_in[:, :, WIDTH : 2 * WIDTH], w_in[:, :, 2 * WIDTH :]]
    parts = [jnp.pad(p, [(0, 0), (0, 4), (0, -p.shape[2] % 8)]) for p in parts]
    w_in = jnp.concatenate(parts, 2).reshape(528, -1)
    w_st = jnp.pad(gru_hidden.T.reshape(3, WIDTH, WIDTH), [(0, 0), (0, 4), (0, 4)]).reshape(528, 176)
    b_in = rows(gru_in_bias.reshape(3, WIDTH), 176).reshape(528, 1)
    b_st = rows(gru_hid_bias.reshape(3, WIDTH), 176).reshape(528, 1)
    freq = jnp.pad(time_freq, (0, 4)).reshape(104, 1)
    phase = jnp.pad(time_phase, (0, 4)).reshape(104, 1)
    return freq, phase, w_in, w_st, b_in, b_st


def slab_exchange(value):
    return lax.all_to_all(value, SLAB, 0, 0, tiled=True)


def zh_all(value):
    copies = jnp.broadcast_to(value[None], (ZH, *value.shape))
    return lax.all_to_all(copies, "zh", 0, 0, tiled=True)


def quarters(mem_t, part):
    width = SLOTS // ZH
    return lax.dynamic_slice_in_dim(mem_t, part * width, width, 1)


def placed(pieces, first):
    stacked = jnp.stack(pieces)
    return jnp.concatenate(
        [lax.dynamic_index_in_dim(stacked, (first - p) % ZH, 0, False) for p in range(ZH)], 1
    )


def to_hosts(mem_t):
    zh, y = lax.axis_index("zh"), lax.axis_index("y")
    mine = quarters(mem_t, y)
    pieces = [
        lax.ppermute(
            mine, ("zh", "y"), [(a * ZH + p, (a + p + k) % ZH * ZH + a) for a in range(ZH) for p in range(ZH)]
        )
        for k in range(ZH)
    ]
    return placed(pieces, zh - y)


def to_homes(sent):
    zh, y = lax.axis_index("zh"), lax.axis_index("y")
    came = [
        lax.ppermute(sent, ("zh", "y"), [(a * ZH + a, a * ZH + (a + k) % ZH) for a in range(ZH)])
        for k in range(1, ZH)
    ]
    return jnp.where(zh == y, sent, sum(came[1:], came[0]))


def body(
    memory,
    node_slot,
    event_nodes,
    event_times,
    valid_mask,
    time_freq,
    time_phase,
    gru_input,
    gru_hidden,
    gru_in_bias,
    gru_hid_bias,
    w_self,
    w_nbr,
    b_embed,
    w_dec1,
    b_dec1,
    w_dec2,
    b_dec2,
):
    zh = jnp.full((1, 1), lax.axis_index("zh"), I32)
    table = node_slot.reshape(512, 128)
    by_column = event_nodes.transpose(0, 2, 1)
    shared = jnp.concatenate([by_column[:, 0:2].reshape(4, EVENTS), event_times, event_times], 0)
    everyone = zh_all(shared)
    ids, times = [], []
    for b in range(2):
        pairs = everyone[:, 2 * b : 2 * b + 2].reshape(8, EVENTS)
        ids.append(jnp.concatenate([pairs, by_column[b, 2:], by_column[b, 2:3]], 0))
        times.append(everyone[:, 4 + b])

    mem_t = to_hosts(memory.T)
    weights = gru_weights(gru_input, gru_hidden, gru_in_bias, gru_hid_bias, time_freq, time_phase)

    def wide(a, to):
        a = a.reshape(-1, a.shape[-1])
        return jnp.pad(a, [(0, to - a.shape[0]), (0, 128 - a.shape[1])])

    params = jnp.concatenate(
        [
            wide(w_self, 176),
            wide(w_nbr, 176),
            wide(w_dec1[:EMBED], 104),
            wide(w_dec1[EMBED:], 104),
            wide(b_embed, 1),
            wide(b_dec1, 1),
            wide(w_dec2, 1),
            wide(b_dec2, 5),
        ],
        0,
    )

    req0, group0, place0, slot0 = route(ids[0], table)
    want0 = slab_exchange(req0.reshape(OWNERS, 1, 128)).reshape(OWNERS, 128)
    req1, group1, place1, slot1 = route(ids[1], table)
    flat0 = group0[:, :ROWS].reshape(-1, 128)
    flat1 = group1[:, :ROWS].reshape(-1, 128)
    plus = req1 + 32
    riding = jnp.pad(
        jnp.stack([plus >> 5, plus & 31], 1).astype(F32).astype(BF), [(0, 0), (0, 6), (0, 0)]
    )
    rows0 = slab_exchange(gather(want0, mem_t, riding, False))
    came = rows0[:, ROWS + HALF : ROWS + HALF + 2, :].astype(F32)
    want1 = (came[:, 0] * 32.0 + came[:, 1]).astype(I32) - 32

    sent0 = loss_and_letters(rows0, flat0, place0, slot0, times[0], zh, valid_mask[0:1], params, False)[0]
    got0 = slab_exchange(sent0)
    mem_t, seen = gru(got0, mem_t, jnp.zeros((1, SLOTS), F32), weights, False)

    def chunk_total(got):
        part = jnp.sum(got[:, PAIR + CHUNK :, :].astype(F32), 0)
        return jnp.sum(zh_all(part), 0)

    total0 = chunk_total(got0)
    hi = lax.reduce_precision(total0, 8, 7)
    low = (total0 - hi).astype(BF)
    hi = hi.astype(BF)
    rows1 = slab_exchange(gather(want1, mem_t, jnp.concatenate([hi, low], 0), True))
    sent1, params, prev = loss_and_letters(
        rows1, flat1, place1, slot1, times[1], zh, valid_mask[1:2], params, True
    )
    got1 = slab_exchange(sent1)
    total1 = chunk_total(got1)
    whole = slab_exchange(jnp.broadcast_to(total1.reshape(1, 2, CHUNK * 64), (OWNERS, 2, CHUNK * 64)))
    final = to_homes(gru(got1, mem_t, seen, weights, True)[0])
    memory_out = jnp.where(final[WIDTH : WIDTH + 1] > 0, final[:WIDTH].astype(F32), memory.T).T
    losses, ws, wn, be, wd, b1, w2, b2 = call(
        final_kernel,
        (
            sds((1, 2), F32),
            sds((WIDTH, EMBED), F32),
            sds((WIDTH, EMBED), F32),
            sds((1, EMBED), F32),
            sds((2 * EMBED, EMBED), F32),
            sds((1, EMBED), F32),
            sds((1, EMBED), F32),
            sds((1, 1), F32),
        ),
        whole.reshape(OWNERS, CHUNK, 128),
        params,
        prev,
    )
    return (
        memory_out,
        losses.reshape(2),
        ws,
        wn,
        be.reshape(EMBED),
        wd,
        b1.reshape(EMBED),
        w2.reshape(EMBED),
        b2.reshape(1),
    )


def solution(mesh):
    finer = Mesh(mesh.devices.reshape(4, ZH, 2, 2, ZH), ALL)
    return jax.shard_map(
        body,
        mesh=finer,
        in_specs=(P(HOME, None), P(), P(None, ALL, None), P(None, ALL), P(None, ALL)) + (P(),) * 13,
        out_specs=(P(HOME, None),) + (P(),) * 8,
        check_vma=False,
    )
```

```python
import functools

import jax
import jax.numpy as jnp
from jax import lax
from jax.experimental import pallas as pl
from jax.experimental.pallas import tpu as pltpu
from jax.sharding import Mesh
from jax.sharding import PartitionSpec as P

HOME = ("x", "zh", "zl", "c")
SLAB = ("x", "y", "zl", "c")
ALL = ("x", "zh", "zl", "c", "y")
ZH = 4
OWNERS = 64
EVENTS = 128
WIDTH = 172
EMBED = 100
SLOTS = 1024
PAIR = 8 * ZH
ROWS = 112
HALF = 56
LEFT = WIDTH - 128
POSITIONS = OWNERS * ROWS
CHUNK = 16
STEP_DEV = 16
STEP = 4.0
F32 = jnp.float32
BF = jnp.bfloat16
I32 = jnp.int32
AT_NBR, AT_DEC_A, AT_DEC_B, AT_VEC = 176, 352, 456, 560
PARAM_ROWS = 568
GRAD_ROWS = OWNERS * CHUNK


def iota(shape, dim):
    return lax.broadcasted_iota(I32, shape, dim)


def mm(a, b):
    return jnp.dot(a, b, preferred_element_type=F32)


def mm_nt(a, b):
    return lax.dot_general(a, b, (((1,), (1,)), ((), ())), preferred_element_type=F32)


def call(kernel, out_shape, *args, flops=1e8, limit=56, **kw):
    moved = sum(a.size * a.dtype.itemsize for a in args)
    return pl.pallas_call(
        kernel,
        out_shape=out_shape,
        compiler_params=pltpu.CompilerParams(vmem_limit_bytes=limit << 20),
        cost_estimate=pl.CostEstimate(flops=int(flops), bytes_accessed=int(moved), transcendentals=0),
        **kw,
    )(*args)


def sds(shape, dtype):
    return jax.ShapeDtypeStruct(shape, dtype)


def route_kernel(ids_ref, table_ref, req_ref, group_ref, place_ref, slot_ref, table_t):
    t = table_ref[...]
    table_t[0:128, :] = jnp.transpose((t >> 8).astype(F32)).astype(BF)
    table_t[128:256, :] = jnp.transpose((t & 255).astype(F32)).astype(BF)
    upper = (iota((128, 128), 0) < iota((128, 128), 1)).astype(F32)
    both = jnp.concatenate([upper, jnp.ones((128, 128), F32)], 1).astype(BF)
    lane = iota((1, 128), 1)
    acc = jnp.zeros((4 * OWNERS, 128), F32)
    base = jnp.zeros((OWNERS, 128), F32)
    for part in range(5):
        ids = [ids_ref[part * 8 + r : part * 8 + r + 1, :] for r in range(8)]
        rows = 7 if part == 4 else 8
        hot = jnp.concatenate(
            [(iota((512, 128), 0) == (n >> 7)).astype(F32).astype(BF) for n in ids[:rows]], 1
        )
        picked = mm(table_t[...], hot)
        sent = []
        slots = []
        for r in range(rows):
            low = iota((128, 128), 0) == (ids[r] & 127)
            hi = jnp.sum(jnp.where(low, picked[:128, r * 128 : (r + 1) * 128], 0.0), 0, keepdims=True)
            lo = jnp.sum(jnp.where(low, picked[128:, r * 128 : (r + 1) * 128], 0.0), 0, keepdims=True)
            slot = (hi * 256.0 + lo).astype(I32)
            slots.append(slot & (SLOTS - 1))
            sent.append(slot >> 10)
        own = [iota((OWNERS, 128), 0) == d for d in sent]
        own_f = [o.astype(F32) for o in own]
        counted = mm(jnp.concatenate([o.astype(BF) for o in own_f], 0), both)
        for r in range(rows):
            mine = counted[r * OWNERS : (r + 1) * OWNERS]
            if part == 0 and r % 2 == 0:
                base = jnp.zeros((OWNERS, 128), F32)
            if part == 1 and r == 0:
                base = jnp.zeros((OWNERS, 128), F32)
            rank = jnp.sum(own_f[r] * (mine[:, :128] + base), 0, keepdims=True).astype(I32)
            base = base + mine[:, 128:]
            plus = slots[r] + 1
            if part == 0:
                where = (r // 2) * 8 + rank
                place_ref[r : r + 1, :] = sent[r] * 8 + rank
                slot_ref[r : r + 1, :] = plus
                ghi = glo = jnp.zeros((1, 128), F32)
            else:
                where = PAIR + rank
                row = (part - 1) * 8 + r
                kind = 3 if row == 0 else (row - 1) // 10
                ghi = jnp.full((1, 128), float(kind + 1), F32)
                glo = lane.astype(F32)
            at = (iota((128, 128), 0) == where).astype(F32).astype(BF)
            planes = [(slots[r] >> 5).astype(F32) + 1.0, (slots[r] & 31).astype(F32), ghi, glo]
            left = jnp.concatenate([own_f[r] * v for v in planes], 0).astype(BF)
            acc = acc + mm_nt(left, at)
    o = OWNERS
    req_ref[...] = ((acc[0:o] - 1.0) * 32.0 + acc[o : 2 * o]).astype(I32)
    group_ref[...] = ((acc[2 * o : 3 * o] - 1.0) * 128.0 + acc[3 * o :]).astype(I32)


def route(ids, table):
    return call(
        route_kernel,
        (sds((OWNERS, 128), I32), sds((OWNERS, 128), I32), sds((8, 128), I32), sds((8, 128), I32)),
        ids,
        table,
        flops=3e9,
        scratch_shapes=[pltpu.VMEM((256, 512), BF)],
    )


def gather_kernel(want_ref, mem_ref, extra_ref, out_ref, mem_rows, *, shared):
    @pl.when(pl.program_id(0) == 0)
    def _():
        m = jnp.concatenate([mem_ref[...], jnp.zeros((4, SLOTS), F32)], 0)
        mem_rows[:, 0:128] = jnp.transpose(m[0:128]).astype(BF)
        tail = jnp.concatenate([m[128:], jnp.zeros((80, SLOTS), F32)], 0)
        mem_rows[:, 128:256] = jnp.transpose(tail).astype(BF)

    cols = jnp.transpose(want_ref[...].astype(F32)).astype(I32)
    lane = iota((ROWS, SLOTS), 1).astype(jnp.int16)

    def hot_of(j):
        col = jnp.broadcast_to(cols[0:ROWS, j : j + 1], (ROWS, 128)).astype(jnp.int16)
        return jnp.where(lane == jnp.concatenate([col] * (SLOTS // 128), 1), BF(1), BF(0))

    rows = mm(jnp.concatenate([hot_of(j) for j in range(STEP_DEV)], 0), mem_rows[...])
    for j in range(STEP_DEV):
        mine = rows[j * ROWS : (j + 1) * ROWS]
        tail = mine[:HALF, 128:] + pltpu.roll(mine[HALF:, 128:], 64, 1)
        extra = extra_ref[...] if shared else extra_ref[j]
        out_ref[j, 0:ROWS, :] = mine[:, :128].astype(BF)
        out_ref[j, ROWS : ROWS + HALF, :] = tail.astype(BF)
        out_ref[j, ROWS + HALF :, :] = extra


def gather(want, mem_t, extra, shared):
    more = extra.shape[-2]
    total = ROWS + HALF + more
    if shared:
        extra_spec = pl.BlockSpec((more, 128), lambda i: (0, 0))
    else:
        extra_spec = pl.BlockSpec((STEP_DEV, more, 128), lambda i: (i, 0, 0))
    return call(
        functools.partial(gather_kernel, shared=shared),
        sds((OWNERS, total, 128), BF),
        want,
        mem_t,
        extra,
        flops=4e9,
        grid=(OWNERS // STEP_DEV,),
        in_specs=[
            pl.BlockSpec((STEP_DEV, 128), lambda i: (i, 0)),
            pl.BlockSpec((WIDTH, SLOTS), lambda i: (0, 0)),
            extra_spec,
        ],
        out_specs=pl.BlockSpec((STEP_DEV, total, 128), lambda i: (i, 0, 0)),
        scratch_shapes=[pltpu.VMEM((SLOTS, 256), BF)],
    )


def stepped(params, grads):
    row, col = iota((PARAM_ROWS, 128), 0), iota((PARAM_ROWS, 128), 1)
    real = (row < AT_VEC + 3) | ((row == AT_VEC + 3) & (col == 0))
    grads = jnp.where(real, grads, 0.0)
    norm = jnp.sqrt(jnp.sum(grads * grads))
    return params - (STEP / (norm + 1e-06)) * grads


def vectors_of(grads):
    return grads[AT_VEC : AT_VEC + 8] + grads[AT_VEC + 8 : AT_VEC + 16] + grads[AT_VEC + 16 : AT_VEC + 24]


def joined(flat):
    return jnp.concatenate([flat[:AT_VEC], vectors_of(flat)], 0)


def softplus(x):
    return jnp.maximum(x, 0.0) + jnp.log1p(jnp.exp(-jnp.abs(x)))


def loss_kernel(*refs, update):
    (rows_ref, group_ref, place_ref, slot_ref, time_ref, zh_ref, valid_ref, param_ref), outs = refs[:8], refs[8:]
    if update:
        out_ref, param_out_ref, prev_ref, rows256, select = outs
        got = rows_ref[:, ROWS + HALF :, :].astype(F32)
        flat = (got[:, :CHUNK] + got[:, CHUNK:]).reshape(GRAD_ROWS, 128)
        grads = joined(flat)
        params = stepped(param_ref[...], grads)
        param_out_ref[...] = params
        prev_ref[...] = grads[AT_VEC:]
    else:
        out_ref, rows256, select = outs
        params = param_ref[...]

    rows256[:, :, 0:128] = rows_ref[:, 0:ROWS, :]
    tails = rows_ref[:, ROWS : ROWS + HALF, :]
    rows256[:, 0:HALF, 128:256] = tails
    rows256[:, HALF:ROWS, 128:256] = pltpu.roll(tails.astype(F32), 64, 2).astype(BF)

    codes = iota((512, 128), 0).astype(jnp.int16)
    for t in range(POSITIONS // 128):
        wanted = jnp.broadcast_to(group_ref[t : t + 1, :], (512, 128)).astype(jnp.int16)
        select[:, t * 128 : (t + 1) * 128] = jnp.where(codes == wanted, BF(1), BF(0))
    summed = mm(select[...], rows256[...].reshape(POSITIONS, 256))
    nbr = summed[: 3 * EVENTS]

    lane256 = iota((EVENTS, 256), 1)
    place = place_ref[...]
    place_c = jnp.transpose(place.astype(F32)).astype(I32)
    plus = slot_ref[...]
    time = time_ref[...]
    info = jnp.concatenate(
        [(plus >> 5).astype(F32), (plus & 31).astype(F32), (time >> 5).astype(F32), (time & 31).astype(F32)], 0
    )
    info_c = jnp.transpose(info)

    tails_out = []
    own = []
    for d in range(ZH):
        held = rows256[:, d * 8 : (d + 1) * 8, :].reshape(OWNERS * 8, 256)
        picked = []
        spread = []
        marked = []
        for c in range(2):
            r = 2 * d + c
            take = (iota((EVENTS, OWNERS * 8), 1) == place_c[:, r : r + 1]).astype(F32).astype(BF)
            x = mm(take, held)
            picked.append(jnp.where(lane256 < WIDTH, x, 0.0))
            spread.append((iota((OWNERS * 8, EVENTS), 0) == place[r : r + 1, :]).astype(F32).astype(BF))
            marks = jnp.zeros((EVENTS, 256), F32)
            for k, col in enumerate((r, 8 + r, 16 + d, 20 + d)):
                marks = jnp.where(lane256 == WIDTH + k, info_c[:, col : col + 1], marks)
            marked.append(marks)
        to_first = (picked[1] + marked[0]).astype(BF)
        to_second = (picked[0] + marked[1]).astype(BF)
        letters = mm(spread[0], to_first) + mm(spread[1], to_second)
        out_ref[:, d * 8 : (d + 1) * 8, :] = letters[:, :128].reshape(OWNERS, 8, 128).astype(BF)
        tails_out.append(letters[:, 128:])
        mine = (zh_ref[...] == d).astype(F32)
        own = [p * mine if d == 0 else o + p * mine for p, o in zip(picked, own or picked)]
    for d in range(2):
        tail = tails_out[d] + pltpu.roll(tails_out[d + 2], 64, 1)
        out_ref[:, PAIR + d * 8 : PAIR + (d + 1) * 8, :] = tail.reshape(OWNERS, 8, 128).astype(BF)

    own_rows = jnp.concatenate(own + [jnp.where(lane256 < WIDTH, summed[3 * EVENTS :], 0.0)], 0).astype(BF)
    zeros = jnp.zeros((80, 128), F32)
    w_self = jnp.concatenate([params[0:AT_NBR], zeros], 0).astype(BF)
    w_nbr = jnp.concatenate([params[AT_NBR:AT_DEC_A], zeros], 0).astype(BF)
    pad = jnp.zeros((24, 128), F32)
    dec_a = jnp.concatenate([params[AT_DEC_A:AT_DEC_B], pad], 0).astype(BF)
    dec_b = jnp.concatenate([params[AT_DEC_B:AT_VEC], pad], 0).astype(BF)
    b_embed = params[AT_VEC : AT_VEC + 1]
    b_dec1 = params[AT_VEC + 1 : AT_VEC + 2]
    w_dec2 = params[AT_VEC + 2 : AT_VEC + 3]
    b_dec2 = params[AT_VEC + 3 : AT_VEC + 4, 0:1]
    nbr_hi = nbr.astype(BF)
    nbr_lo = (nbr - nbr_hi.astype(F32)).astype(BF)
    mean = (mm(nbr_hi, w_nbr) + mm(nbr_lo, w_nbr)) * 0.1
    act = jnp.tanh(mm(own_rows, w_self) + mean + b_embed)
    hidden = act.astype(BF)
    first = jnp.concatenate([hidden[:EVENTS], hidden[:EVENTS]], 0)
    second = hidden[EVENTS:]
    pre = mm(first, dec_a) + mm(second, dec_b) + b_dec1
    inner = jnp.maximum(pre, 0.0)
    logits = jnp.sum(inner * w_dec2, 1, keepdims=True) + b_dec2
    valid_row = valid_ref[...].astype(F32)
    valid = jnp.transpose(jnp.broadcast_to(valid_row, (128, 128)))[:, 0:1]
    valid = jnp.concatenate([valid, valid], 0)
    sign = jnp.where(iota((2 * EVENTS, 1), 0) < EVENTS, -1.0, 1.0)
    loss = jnp.sum(softplus(sign * logits) * valid)
    count = jnp.sum(valid_row)
    d_logit = sign * jax.nn.sigmoid(sign * logits) * valid
    d_inner = jnp.where(pre > 0.0, d_logit * w_dec2, 0.0)
    d_bf = d_inner.astype(BF)
    g_dec2 = jnp.sum(inner * d_logit, 0, keepdims=True)
    g_b2 = jnp.sum(d_logit)
    g_b1 = jnp.sum(d_inner, 0, keepdims=True)
    d_first = mm_nt(d_bf, dec_a).astype(BF).astype(F32)
    d_second = mm_nt(d_bf, dec_b).astype(BF).astype(F32)
    d_zero = (d_first[:EVENTS] + d_first[EVENTS:]).astype(BF).astype(F32)
    d_pre = jnp.concatenate([d_zero, d_second], 0) * (1.0 - act * act)
    g_be = jnp.sum(d_pre, 0, keepdims=True)

    def mm_tn(a, b):
        return mm(jnp.transpose(a.astype(F32)).astype(BF), b)

    g_self = mm_tn(own_rows, d_pre.astype(BF))[:176]
    d_mean = (d_pre * 0.1).astype(BF)
    g_nbr = (mm_tn(nbr_hi, d_mean) + mm_tn(nbr_lo, d_mean))[:176]
    g_nbr = jnp.where(iota((176, 128), 0) < WIDTH, g_nbr, 0.0)
    g_a = mm_tn(first, d_bf)[:104]
    g_b = mm_tn(second, d_bf)[:104]
    one = jnp.ones((1, 128), F32)
    vec = jnp.concatenate([g_be, g_b1, g_dec2, g_b2 * one, loss * one, count * one, one * 0.0, one * 0.0], 0)
    hi = vec.astype(BF).astype(F32)
    mid = (vec - hi).astype(BF).astype(F32)
    low = vec - hi - mid
    rest = jnp.zeros((GRAD_ROWS - AT_VEC - 24, 128), F32)
    grads = jnp.concatenate([g_self, g_nbr, g_a, g_b, hi, mid, low, rest], 0)
    out_ref[:, PAIR + CHUNK :, :] = grads.reshape(OWNERS, CHUNK, 128).astype(BF)


def loss_and_letters(rows, group, place, slot, time, zh, valid, params, update):
    out = [sds((OWNERS, PAIR + CHUNK + CHUNK, 128), BF)]
    if update:
        out += [sds((PARAM_ROWS, 128), F32), sds((8, 128), F32)]
    return call(
        functools.partial(loss_kernel, update=update),
        tuple(out),
        rows,
        group,
        place,
        slot,
        time,
        zh,
        valid,
        params,
        flops=1e10,
        limit=40,
        scratch_shapes=[pltpu.VMEM((OWNERS, ROWS, 256), BF), pltpu.VMEM((512, POSITIONS), BF)],
    )


def final_kernel(got_ref, param_ref, prev_ref, loss_ref, ws_ref, wn_ref, be_ref, wd_ref, b1_ref, w2_ref, b2_ref):
    grads = joined(got_ref[...].reshape(GRAD_ROWS, 128))
    params = stepped(param_ref[...], grads)
    vec = grads[AT_VEC:]
    prev = prev_ref[...]
    first = prev[4:5] / jnp.maximum(prev[5:6], 1.0)
    second = vec[4:5] / jnp.maximum(vec[5:6], 1.0)
    loss_ref[...] = jnp.where(iota((1, 128), 1) == 0, first, second)[:, 0:2]
    ws_ref[...] = params[0:WIDTH, :EMBED]
    wn_ref[...] = params[AT_NBR : AT_NBR + WIDTH, :EMBED]
    wd_ref[0:EMBED, :] = params[AT_DEC_A : AT_DEC_A + EMBED, :EMBED]
    wd_ref[EMBED:, :] = params[AT_DEC_B : AT_DEC_B + EMBED, :EMBED]
    be_ref[...] = params[AT_VEC : AT_VEC + 1, :EMBED]
    b1_ref[...] = params[AT_VEC + 1 : AT_VEC + 2, :EMBED]
    w2_ref[...] = params[AT_VEC + 2 : AT_VEC + 3, :EMBED]
    b2_ref[...] = params[AT_VEC + 3 : AT_VEC + 4, 0:1]


def gru_kernel(
    got_ref, mem_ref, seen_ref, freq_ref, phase_ref, w_in_ref, w_st_ref, b_in_ref, b_st_ref, *outs, last
):
    hot, stack = outs[-2:]
    half = PAIR // 2
    for h in range(2):
        n = OWNERS * half
        head = got_ref[:, h * half : (h + 1) * half, :].reshape(n, 128).astype(F32)
        tail = got_ref[:, PAIR : PAIR + half, :].reshape(n, 128).astype(F32)
        if h:
            tail = pltpu.roll(tail, 64, 1)
        col = (tail[:, LEFT : LEFT + 1] * 32.0 + tail[:, LEFT + 1 : LEFT + 2]).astype(I32) - 1
        col = jnp.broadcast_to(col, (n, 128)).astype(jnp.int16)
        slots = iota((n, SLOTS), 1).astype(jnp.int16)
        hot[h * n : (h + 1) * n, :] = jnp.where(slots == jnp.concatenate([col] * (SLOTS // 128), 1), BF(1), BF(0))
        here = pl.ds(h * n, n)
        tail_t = jnp.transpose(tail)[0:48]
        when = tail_t[46:47] * 32.0 + tail_t[47:48]
        code = jnp.cos(freq_ref[...] * when + phase_ref[...])
        stack[0:128, here] = jnp.transpose(head).astype(BF)
        stack[128:176, here] = jnp.where(iota((48, n), 0) == LEFT, 1.0, tail_t).astype(BF)
        stack[176:280, here] = code.astype(BF)
    summed = mm(stack[...], hot[...])
    counts = summed[WIDTH : WIDTH + 1]
    mean = (summed / jnp.maximum(counts, 1.0)).astype(BF)
    mem = mem_ref[...]
    mem_pad = jnp.concatenate([mem, jnp.zeros((4, SLOTS), F32)], 0)
    state = mem_pad.astype(BF)
    from_in = mm(w_in_ref[...], jnp.concatenate([state, mean], 0)) + b_in_ref[...]
    from_st = mm(w_st_ref[...], state) + b_st_ref[...]
    reset = jax.nn.sigmoid(from_in[0:176] + from_st[0:176])
    update = jax.nn.sigmoid(from_in[176:352] + from_st[176:352])
    candidate = jnp.tanh(from_in[352:528] + reset * from_st[352:528])
    fresh = (1.0 - update) * candidate + update * mem_pad
    new = jnp.where(counts > 0.0, fresh, mem_pad)
    seen = jnp.maximum(counts, seen_ref[...])
    if last:
        flag = jnp.minimum(seen, 1.0)
        outs[0][...] = jnp.where(iota((176, SLOTS), 0) == WIDTH, flag, new).astype(BF)
    else:
        outs[0][...] = new[:WIDTH]
        outs[1][...] = seen


def gru(got, mem_t, seen, weights, last):
    n = OWNERS * PAIR
    if last:
        out = (sds((176, SLOTS), BF),)
    else:
        out = (sds((WIDTH, SLOTS), F32), sds((1, SLOTS), F32))
    return call(
        functools.partial(gru_kernel, last=last),
        out,
        got,
        mem_t,
        seen,
        *weights,
        flops=3e9,
        limit=40,
        scratch_shapes=[pltpu.VMEM((n, SLOTS), BF), pltpu.VMEM((280, n), BF)],
    )


def gru_weights(gru_input, gru_hidden, gru_in_bias, gru_hid_bias, time_freq, time_phase):
    def rows(a, to):
        return jnp.pad(a, [(0, 0), (0, to - a.shape[1])] + [(0, 0)] * (a.ndim - 2))

    w_in = gru_input.T.reshape(3, WIDTH, -1)
    parts = [w_in[:, :, :WIDTH], w_in[:, :, WIDTH : 2 * WIDTH], w_in[:, :, 2 * WIDTH :]]
    parts = [jnp.pad(p, [(0, 0), (0, 4), (0, -p.shape[2] % 8)]) for p in parts]
    w_in = jnp.concatenate(parts, 2).reshape(528, -1)
    w_st = jnp.pad(gru_hidden.T.reshape(3, WIDTH, WIDTH), [(0, 0), (0, 4), (0, 4)]).reshape(528, 176)
    b_in = rows(gru_in_bias.reshape(3, WIDTH), 176).reshape(528, 1)
    b_st = rows(gru_hid_bias.reshape(3, WIDTH), 176).reshape(528, 1)
    freq = jnp.pad(time_freq, (0, 4)).reshape(104, 1)
    phase = jnp.pad(time_phase, (0, 4)).reshape(104, 1)
    return freq, phase, w_in, w_st, b_in, b_st


def slab_exchange(value):
    return lax.all_to_all(value, SLAB, 0, 0, tiled=True)


def zh_all(value):
    copies = jnp.broadcast_to(value[None], (ZH, *value.shape))
    return lax.all_to_all(copies, "zh", 0, 0, tiled=True)


def to_hosts(mem_t):
    zh, y = lax.axis_index("zh"), lax.axis_index("y")
    width = SLOTS // 2
    mine = lax.dynamic_slice_in_dim(mem_t, y // 2 * width, width, 1)
    came = [
        lax.ppermute(
            mine, ("zh", "y"), [(a * ZH + p, (a + p + k) % ZH * ZH + a) for a in range(ZH) for p in range(ZH)]
        )
        for k in (0, 2)
    ]
    straight = (zh - y) % ZH < 2
    low = jnp.where(straight, came[0], came[1])
    high = jnp.where(straight, came[1], came[0])
    return jnp.concatenate([low, high], 1)


def to_homes(sent):
    zh, y = lax.axis_index("zh"), lax.axis_index("y")
    came = [
        lax.ppermute(sent, ("zh", "y"), [(a * ZH + a, a * ZH + (a + k) % ZH) for a in range(ZH)])
        for k in range(1, ZH)
    ]
    return jnp.where(zh == y, sent, sum(came[1:], came[0]))


def body(
    memory,
    node_slot,
    event_nodes,
    event_times,
    valid_mask,
    time_freq,
    time_phase,
    gru_input,
    gru_hidden,
    gru_in_bias,
    gru_hid_bias,
    w_self,
    w_nbr,
    b_embed,
    w_dec1,
    b_dec1,
    w_dec2,
    b_dec2,
):
    zh = jnp.full((1, 1), lax.axis_index("zh"), I32)
    table = node_slot.reshape(512, 128)
    by_column = event_nodes.transpose(0, 2, 1)
    shared = jnp.concatenate([by_column[:, 0:2].reshape(4, EVENTS), event_times, event_times], 0)
    everyone = zh_all(shared)
    ids, times = [], []
    for b in range(2):
        pairs = everyone[:, 2 * b : 2 * b + 2].reshape(8, EVENTS)
        ids.append(jnp.concatenate([pairs, by_column[b, 2:], by_column[b, 2:3]], 0))
        times.append(everyone[:, 4 + b])

    mem_t, _ = lax.optimization_barrier((memory.T, everyone))
    mem_t = to_hosts(mem_t)
    weights = gru_weights(gru_input, gru_hidden, gru_in_bias, gru_hid_bias, time_freq, time_phase)

    def wide(a, to):
        a = a.reshape(-1, a.shape[-1])
        return jnp.pad(a, [(0, to - a.shape[0]), (0, 128 - a.shape[1])])

    params = jnp.concatenate(
        [
            wide(w_self, 176),
            wide(w_nbr, 176),
            wide(w_dec1[:EMBED], 104),
            wide(w_dec1[EMBED:], 104),
            wide(b_embed, 1),
            wide(b_dec1, 1),
            wide(w_dec2, 1),
            wide(b_dec2, 5),
        ],
        0,
    )

    req0, group0, place0, slot0 = route(ids[0], table)
    want0 = slab_exchange(req0.reshape(OWNERS, 1, 128)).reshape(OWNERS, 128)
    later, mem_t = lax.optimization_barrier((ids[1], mem_t))
    req1, group1, place1, slot1 = route(later, table)
    flat0 = group0[:, :ROWS].reshape(-1, 128)
    flat1 = group1[:, :ROWS].reshape(-1, 128)
    plus = req1 + 32
    riding = jnp.pad(
        jnp.stack([plus >> 5, plus & 31], 1).astype(F32).astype(BF), [(0, 0), (0, 6), (0, 0)]
    )
    rows0 = slab_exchange(gather(want0, mem_t, riding, False))
    came = rows0[:, ROWS + HALF : ROWS + HALF + 2, :].astype(F32)
    want1 = (came[:, 0] * 32.0 + came[:, 1]).astype(I32) - 32

    sent0 = loss_and_letters(rows0, flat0, place0, slot0, times[0], zh, valid_mask[0:1], params, False)[0]
    got0 = slab_exchange(sent0)
    mem_t, seen = gru(got0, mem_t, jnp.zeros((1, SLOTS), F32), weights, False)

    def chunk_total(got):
        part = jnp.sum(got[:, PAIR + CHUNK :, :].astype(F32), 0)
        return jnp.sum(zh_all(part), 0)

    total0 = chunk_total(got0)
    hi = lax.reduce_precision(total0, 8, 7)
    low = (total0 - hi).astype(BF)
    hi = hi.astype(BF)
    rows1 = slab_exchange(gather(want1, mem_t, jnp.concatenate([hi, low], 0), True))
    sent1, params, prev = loss_and_letters(
        rows1, flat1, place1, slot1, times[1], zh, valid_mask[1:2], params, True
    )
    got1 = slab_exchange(sent1)
    total1, last = lax.optimization_barrier((chunk_total(got1), gru(got1, mem_t, seen, weights, True)[0]))
    whole = slab_exchange(jnp.broadcast_to(total1.reshape(1, 2, CHUNK * 64), (OWNERS, 2, CHUNK * 64)))
    losses, ws, wn, be, wd, b1, w2, b2 = call(
        final_kernel,
        (
            sds((1, 2), F32),
            sds((WIDTH, EMBED), F32),
            sds((WIDTH, EMBED), F32),
            sds((1, EMBED), F32),
            sds((2 * EMBED, EMBED), F32),
            sds((1, EMBED), F32),
            sds((1, EMBED), F32),
            sds((1, 1), F32),
        ),
        whole.reshape(OWNERS, CHUNK, 128),
        params,
        prev,
    )
    final = to_homes(last)
    old, losses = lax.optimization_barrier((memory.T, losses))
    memory_out = jnp.where(final[WIDTH : WIDTH + 1] > 0, final[:WIDTH].astype(F32), old).T
    return (
        memory_out,
        losses.reshape(2),
        ws,
        wn,
        be.reshape(EMBED),
        wd,
        b1.reshape(EMBED),
        w2.reshape(EMBED),
        b2.reshape(1),
    )


def solution(mesh):
    finer = Mesh(mesh.devices.reshape(4, ZH, 2, 2, ZH), ALL)
    return jax.shard_map(
        body,
        mesh=finer,
        in_specs=(P(HOME, None), P(), P(None, ALL, None), P(None, ALL), P(None, ALL)) + (P(),) * 13,
        out_specs=(P(HOME, None),) + (P(),) * 8,
        check_vma=False,
    )
```

```python
import functools

import jax
import jax.numpy as jnp
from jax import lax
from jax.experimental import pallas as pl
from jax.experimental.pallas import tpu as pltpu
from jax.sharding import Mesh
from jax.sharding import PartitionSpec as P

HOME = ("x", "zh", "zl", "c")
SLAB = ("x", "y", "zl", "c")
ALL = ("x", "zh", "zl", "c", "y")
ZH = 4
OWNERS = 64
EVENTS = 128
WIDTH = 172
EMBED = 100
SLOTS = 1024
PAIR = 8 * ZH
ROWS = 112
HALF = 56
LEFT = WIDTH - 128
POSITIONS = OWNERS * ROWS
CHUNK = 16
STEP_DEV = 16
STEP = 4.0
F32 = jnp.float32
BF = jnp.bfloat16
HALF_FLOAT = jnp.float16
RANGE = 8192.0
I32 = jnp.int32
AT_NBR, AT_DEC_A, AT_DEC_B, AT_VEC = 176, 352, 456, 560
PARAM_ROWS = 568
GRAD_ROWS = OWNERS * CHUNK


def iota(shape, dim):
    return lax.broadcasted_iota(I32, shape, dim)


def mm(a, b):
    return jnp.dot(a, b, preferred_element_type=F32)


def mm_nt(a, b):
    return lax.dot_general(a, b, (((1,), (1,)), ((), ())), preferred_element_type=F32)


def call(kernel, out_shape, *args, flops=1e8, limit=56, **kw):
    moved = sum(a.size * a.dtype.itemsize for a in args)
    return pl.pallas_call(
        kernel,
        out_shape=out_shape,
        compiler_params=pltpu.CompilerParams(vmem_limit_bytes=limit << 20),
        cost_estimate=pl.CostEstimate(flops=int(flops), bytes_accessed=int(moved), transcendentals=0),
        **kw,
    )(*args)


def sds(shape, dtype):
    return jax.ShapeDtypeStruct(shape, dtype)


def route_kernel(ids_ref, table_ref, req_ref, group_ref, place_ref, slot_ref, table_t):
    t = table_ref[...]
    table_t[0:128, :] = jnp.transpose((t >> 8).astype(F32)).astype(BF)
    table_t[128:256, :] = jnp.transpose((t & 255).astype(F32)).astype(BF)
    upper = (iota((128, 128), 0) < iota((128, 128), 1)).astype(F32)
    both = jnp.concatenate([upper, jnp.ones((128, 128), F32)], 1).astype(BF)
    lane = iota((1, 128), 1)
    acc = jnp.zeros((4 * OWNERS, 128), F32)
    base = jnp.zeros((OWNERS, 128), F32)
    for part in range(5):
        ids = [ids_ref[part * 8 + r : part * 8 + r + 1, :] for r in range(8)]
        rows = 7 if part == 4 else 8
        hot = jnp.concatenate(
            [(iota((512, 128), 0) == (n >> 7)).astype(F32).astype(BF) for n in ids[:rows]], 1
        )
        picked = mm(table_t[...], hot)
        sent = []
        slots = []
        for r in range(rows):
            low = iota((128, 128), 0) == (ids[r] & 127)
            hi = jnp.sum(jnp.where(low, picked[:128, r * 128 : (r + 1) * 128], 0.0), 0, keepdims=True)
            lo = jnp.sum(jnp.where(low, picked[128:, r * 128 : (r + 1) * 128], 0.0), 0, keepdims=True)
            slot = (hi * 256.0 + lo).astype(I32)
            slots.append(slot & (SLOTS - 1))
            sent.append(slot >> 10)
        own = [iota((OWNERS, 128), 0) == d for d in sent]
        own_f = [o.astype(F32) for o in own]
        counted = mm(jnp.concatenate([o.astype(BF) for o in own_f], 0), both)
        for r in range(rows):
            mine = counted[r * OWNERS : (r + 1) * OWNERS]
            if part == 0 and r % 2 == 0:
                base = jnp.zeros((OWNERS, 128), F32)
            if part == 1 and r == 0:
                base = jnp.zeros((OWNERS, 128), F32)
            rank = jnp.sum(own_f[r] * (mine[:, :128] + base), 0, keepdims=True).astype(I32)
            base = base + mine[:, 128:]
            plus = slots[r] + 1
            if part == 0:
                where = (r // 2) * 8 + rank
                place_ref[r : r + 1, :] = sent[r] * 8 + rank
                slot_ref[r : r + 1, :] = plus
                ghi = glo = jnp.zeros((1, 128), F32)
            else:
                where = PAIR + rank
                row = (part - 1) * 8 + r
                kind = 3 if row == 0 else (row - 1) // 10
                ghi = jnp.full((1, 128), float(kind + 1), F32)
                glo = lane.astype(F32)
            at = (iota((128, 128), 0) == where).astype(F32).astype(BF)
            planes = [(slots[r] >> 5).astype(F32) + 1.0, (slots[r] & 31).astype(F32), ghi, glo]
            left = jnp.concatenate([own_f[r] * v for v in planes], 0).astype(BF)
            acc = acc + mm_nt(left, at)
    o = OWNERS
    req_ref[...] = ((acc[0:o] - 1.0) * 32.0 + acc[o : 2 * o]).astype(I32)
    group_ref[...] = ((acc[2 * o : 3 * o] - 1.0) * 128.0 + acc[3 * o :]).astype(I32)


def route(ids, table):
    return call(
        route_kernel,
        (sds((OWNERS, 128), I32), sds((OWNERS, 128), I32), sds((8, 128), I32), sds((8, 128), I32)),
        ids,
        table,
        flops=3e9,
        scratch_shapes=[pltpu.VMEM((256, 512), BF)],
    )


def gather_kernel(want_ref, mem_ref, extra_ref, out_ref, mem_rows, *, shared):
    @pl.when(pl.program_id(0) == 0)
    def _():
        m = jnp.concatenate([mem_ref[...], jnp.zeros((4, SLOTS), F32)], 0)
        mem_rows[:, 0:128] = jnp.transpose(m[0:128]).astype(BF)
        tail = jnp.concatenate([m[128:], jnp.zeros((80, SLOTS), F32)], 0)
        mem_rows[:, 128:256] = jnp.transpose(tail).astype(BF)

    cols = jnp.transpose(want_ref[...].astype(F32)).astype(I32)
    lane = iota((ROWS, SLOTS), 1).astype(jnp.int16)

    def hot_of(j):
        col = jnp.broadcast_to(cols[0:ROWS, j : j + 1], (ROWS, 128)).astype(jnp.int16)
        return jnp.where(lane == jnp.concatenate([col] * (SLOTS // 128), 1), BF(1), BF(0))

    rows = mm(jnp.concatenate([hot_of(j) for j in range(STEP_DEV)], 0), mem_rows[...])
    for j in range(STEP_DEV):
        mine = rows[j * ROWS : (j + 1) * ROWS]
        tail = mine[:HALF, 128:] + pltpu.roll(mine[HALF:, 128:], 64, 1)
        extra = extra_ref[...] if shared else extra_ref[j]
        out_ref[j, 0:ROWS, :] = mine[:, :128].astype(BF)
        out_ref[j, ROWS : ROWS + HALF, :] = tail.astype(BF)
        out_ref[j, ROWS + HALF :, :] = extra


def gather(want, mem_t, extra, shared):
    more = extra.shape[-2]
    total = ROWS + HALF + more
    if shared:
        extra_spec = pl.BlockSpec((more, 128), lambda i: (0, 0))
    else:
        extra_spec = pl.BlockSpec((STEP_DEV, more, 128), lambda i: (i, 0, 0))
    return call(
        functools.partial(gather_kernel, shared=shared),
        sds((OWNERS, total, 128), BF),
        want,
        mem_t,
        extra,
        flops=4e9,
        limit=28,
        grid=(OWNERS // STEP_DEV,),
        in_specs=[
            pl.BlockSpec((STEP_DEV, 128), lambda i: (i, 0)),
            pl.BlockSpec((WIDTH, SLOTS), lambda i: (0, 0)),
            extra_spec,
        ],
        out_specs=pl.BlockSpec((STEP_DEV, total, 128), lambda i: (i, 0, 0)),
        scratch_shapes=[pltpu.VMEM((SLOTS, 256), BF)],
    )


def stepped(params, grads):
    row, col = iota((PARAM_ROWS, 128), 0), iota((PARAM_ROWS, 128), 1)
    real = (row < AT_VEC + 3) | ((row == AT_VEC + 3) & (col == 0))
    grads = jnp.where(real, grads, 0.0)
    norm = jnp.sqrt(jnp.sum(grads * grads))
    return params - (STEP / (norm + 1e-06)) * grads


def vectors_of(grads):
    return grads[AT_VEC : AT_VEC + 8] + grads[AT_VEC + 8 : AT_VEC + 16] + grads[AT_VEC + 16 : AT_VEC + 24]


def joined(flat):
    return jnp.concatenate([flat[:AT_VEC], vectors_of(flat)], 0)


def softplus(x):
    return jnp.maximum(x, 0.0) + jnp.log1p(jnp.exp(-jnp.abs(x)))


def loss_kernel(*refs, update):
    (rows_ref, group_ref, place_ref, slot_ref, time_ref, zh_ref, valid_ref, param_ref), outs = refs[:8], refs[8:]
    if update:
        out_ref, param_out_ref, prev_ref, rows256, select = outs
        got = rows_ref[:, ROWS + HALF :, :].astype(F32)
        flat = (got[:, :CHUNK] + got[:, CHUNK:]).reshape(GRAD_ROWS, 128)
        grads = joined(flat)
        params = stepped(param_ref[...], grads)
        param_out_ref[...] = params
        prev_ref[...] = grads[AT_VEC:]
    else:
        out_ref, rows256, select = outs
        params = param_ref[...]

    rows256[:, :, 0:128] = rows_ref[:, 0:ROWS, :]
    tails = rows_ref[:, ROWS : ROWS + HALF, :]
    rows256[:, 0:HALF, 128:256] = tails
    rows256[:, HALF:ROWS, 128:256] = pltpu.roll(tails.astype(F32), 64, 2).astype(BF)

    codes = iota((512, 128), 0).astype(jnp.int16)
    for t in range(POSITIONS // 128):
        wanted = jnp.broadcast_to(group_ref[t : t + 1, :], (512, 128)).astype(jnp.int16)
        select[:, t * 128 : (t + 1) * 128] = jnp.where(codes == wanted, BF(1), BF(0))
    summed = mm(select[...], rows256[...].reshape(POSITIONS, 256))
    nbr = summed[: 3 * EVENTS]

    lane256 = iota((EVENTS, 256), 1)
    place = place_ref[...]
    place_c = jnp.transpose(place.astype(F32)).astype(I32)
    plus = slot_ref[...]
    time = time_ref[...]
    info = jnp.concatenate(
        [(plus >> 5).astype(F32), (plus & 31).astype(F32), (time >> 5).astype(F32), (time & 31).astype(F32)], 0
    )
    info_c = jnp.transpose(info)

    tails_out = []
    own = []
    for d in range(ZH):
        held = rows256[:, d * 8 : (d + 1) * 8, :].reshape(OWNERS * 8, 256)
        picked = []
        spread = []
        marked = []
        for c in range(2):
            r = 2 * d + c
            take = (iota((EVENTS, OWNERS * 8), 1) == place_c[:, r : r + 1]).astype(F32).astype(BF)
            x = mm(take, held)
            picked.append(jnp.where(lane256 < WIDTH, x, 0.0))
            spread.append((iota((OWNERS * 8, EVENTS), 0) == place[r : r + 1, :]).astype(F32).astype(BF))
            marks = jnp.zeros((EVENTS, 256), F32)
            for k, col in enumerate((r, 8 + r, 16 + d, 20 + d)):
                marks = jnp.where(lane256 == WIDTH + k, info_c[:, col : col + 1], marks)
            marked.append(marks)
        to_first = (picked[1] + marked[0]).astype(BF)
        to_second = (picked[0] + marked[1]).astype(BF)
        letters = mm(spread[0], to_first) + mm(spread[1], to_second)
        out_ref[:, d * 8 : (d + 1) * 8, :] = letters[:, :128].reshape(OWNERS, 8, 128).astype(BF)
        tails_out.append(letters[:, 128:])
        mine = (zh_ref[...] == d).astype(F32)
        own = [p * mine if d == 0 else o + p * mine for p, o in zip(picked, own or picked)]
    for d in range(2):
        tail = tails_out[d] + pltpu.roll(tails_out[d + 2], 64, 1)
        out_ref[:, PAIR + d * 8 : PAIR + (d + 1) * 8, :] = tail.reshape(OWNERS, 8, 128).astype(BF)

    own_rows = jnp.concatenate(own + [jnp.where(lane256 < WIDTH, summed[3 * EVENTS :], 0.0)], 0).astype(BF)
    zeros = jnp.zeros((80, 128), F32)
    w_self = jnp.concatenate([params[0:AT_NBR], zeros], 0).astype(BF)
    w_nbr = jnp.concatenate([params[AT_NBR:AT_DEC_A], zeros], 0).astype(BF)
    pad = jnp.zeros((24, 128), F32)
    dec_a = jnp.concatenate([params[AT_DEC_A:AT_DEC_B], pad], 0).astype(BF)
    dec_b = jnp.concatenate([params[AT_DEC_B:AT_VEC], pad], 0).astype(BF)
    b_embed = params[AT_VEC : AT_VEC + 1]
    b_dec1 = params[AT_VEC + 1 : AT_VEC + 2]
    w_dec2 = params[AT_VEC + 2 : AT_VEC + 3]
    b_dec2 = params[AT_VEC + 3 : AT_VEC + 4, 0:1]
    nbr_hi = nbr.astype(BF)
    nbr_lo = (nbr - nbr_hi.astype(F32)).astype(BF)
    mean = (mm(nbr_hi, w_nbr) + mm(nbr_lo, w_nbr)) * 0.1
    act = jnp.tanh(mm(own_rows, w_self) + mean + b_embed)
    hidden = act.astype(BF)
    first = jnp.concatenate([hidden[:EVENTS], hidden[:EVENTS]], 0)
    second = hidden[EVENTS:]
    pre = mm(first, dec_a) + mm(second, dec_b) + b_dec1
    inner = jnp.maximum(pre, 0.0)
    logits = jnp.sum(inner * w_dec2, 1, keepdims=True) + b_dec2
    valid_row = valid_ref[...].astype(F32)
    valid = jnp.transpose(jnp.broadcast_to(valid_row, (128, 128)))[:, 0:1]
    valid = jnp.concatenate([valid, valid], 0)
    sign = jnp.where(iota((2 * EVENTS, 1), 0) < EVENTS, -1.0, 1.0)
    loss = jnp.sum(softplus(sign * logits) * valid)
    count = jnp.sum(valid_row)
    d_logit = sign * jax.nn.sigmoid(sign * logits) * valid
    d_inner = jnp.where(pre > 0.0, d_logit * w_dec2, 0.0)
    d_bf = d_inner.astype(BF)
    g_dec2 = jnp.sum(inner * d_logit, 0, keepdims=True)
    g_b2 = jnp.sum(d_logit)
    g_b1 = jnp.sum(d_inner, 0, keepdims=True)
    d_first = mm_nt(d_bf, dec_a).astype(BF).astype(F32)
    d_second = mm_nt(d_bf, dec_b).astype(BF).astype(F32)
    d_zero = (d_first[:EVENTS] + d_first[EVENTS:]).astype(BF).astype(F32)
    d_pre = jnp.concatenate([d_zero, d_second], 0) * (1.0 - act * act)
    g_be = jnp.sum(d_pre, 0, keepdims=True)

    def mm_tn(a, b):
        return mm(jnp.transpose(a.astype(F32)).astype(BF), b)

    g_self = mm_tn(own_rows, d_pre.astype(BF))[:176]
    d_mean = (d_pre * 0.1).astype(BF)
    g_nbr = (mm_tn(nbr_hi, d_mean) + mm_tn(nbr_lo, d_mean))[:176]
    g_nbr = jnp.where(iota((176, 128), 0) < WIDTH, g_nbr, 0.0)
    g_a = mm_tn(first, d_bf)[:104]
    g_b = mm_tn(second, d_bf)[:104]
    one = jnp.ones((1, 128), F32)
    vec = jnp.concatenate([g_be, g_b1, g_dec2, g_b2 * one, loss * one, count * one, one * 0.0, one * 0.0], 0)
    hi = vec.astype(BF).astype(F32)
    mid = (vec - hi).astype(BF).astype(F32)
    low = vec - hi - mid
    rest = jnp.zeros((GRAD_ROWS - AT_VEC - 24, 128), F32)
    grads = jnp.concatenate([g_self, g_nbr, g_a, g_b, hi, mid, low, rest], 0)
    out_ref[:, PAIR + CHUNK :, :] = grads.reshape(OWNERS, CHUNK, 128).astype(BF)


def loss_and_letters(rows, group, place, slot, time, zh, valid, params, update):
    out = [sds((OWNERS, PAIR + CHUNK + CHUNK, 128), BF)]
    if update:
        out += [sds((PARAM_ROWS, 128), F32), sds((8, 128), F32)]
    return call(
        functools.partial(loss_kernel, update=update),
        tuple(out),
        rows,
        group,
        place,
        slot,
        time,
        zh,
        valid,
        params,
        flops=1e10,
        limit=40,
        scratch_shapes=[pltpu.VMEM((OWNERS, ROWS, 256), BF), pltpu.VMEM((512, POSITIONS), BF)],
    )


def final_kernel(got_ref, param_ref, prev_ref, loss_ref, ws_ref, wn_ref, be_ref, wd_ref, b1_ref, w2_ref, b2_ref):
    grads = joined(got_ref[...].reshape(GRAD_ROWS, 128))
    params = stepped(param_ref[...], grads)
    vec = grads[AT_VEC:]
    prev = prev_ref[...]
    first = prev[4:5] / jnp.maximum(prev[5:6], 1.0)
    second = vec[4:5] / jnp.maximum(vec[5:6], 1.0)
    loss_ref[...] = jnp.where(iota((1, 128), 1) == 0, first, second)[:, 0:2]
    ws_ref[...] = params[0:WIDTH, :EMBED]
    wn_ref[...] = params[AT_NBR : AT_NBR + WIDTH, :EMBED]
    wd_ref[0:EMBED, :] = params[AT_DEC_A : AT_DEC_A + EMBED, :EMBED]
    wd_ref[EMBED:, :] = params[AT_DEC_B : AT_DEC_B + EMBED, :EMBED]
    be_ref[...] = params[AT_VEC : AT_VEC + 1, :EMBED]
    b1_ref[...] = params[AT_VEC + 1 : AT_VEC + 2, :EMBED]
    w2_ref[...] = params[AT_VEC + 2 : AT_VEC + 3, :EMBED]
    b2_ref[...] = params[AT_VEC + 3 : AT_VEC + 4, 0:1]


def gru_kernel(
    got_ref, mem_ref, seen_ref, freq_ref, phase_ref, w_in_ref, w_st_ref, b_in_ref, b_st_ref, *outs, last
):
    hot, stack = outs[-2:]
    half = PAIR // 2
    for h in range(2):
        n = OWNERS * half
        head = got_ref[:, h * half : (h + 1) * half, :].reshape(n, 128).astype(F32)
        tail = got_ref[:, PAIR : PAIR + half, :].reshape(n, 128).astype(F32)
        if h:
            tail = pltpu.roll(tail, 64, 1)
        col = (tail[:, LEFT : LEFT + 1] * 32.0 + tail[:, LEFT + 1 : LEFT + 2]).astype(I32) - 1
        col = jnp.broadcast_to(col, (n, 128)).astype(jnp.int16)
        slots = iota((n, SLOTS), 1).astype(jnp.int16)
        hot[h * n : (h + 1) * n, :] = jnp.where(slots == jnp.concatenate([col] * (SLOTS // 128), 1), BF(1), BF(0))
        here = pl.ds(h * n, n)
        tail_t = jnp.transpose(tail)[0:48]
        when = tail_t[46:47] * 32.0 + tail_t[47:48]
        code = jnp.cos(freq_ref[...] * when + phase_ref[...])
        stack[0:128, here] = jnp.transpose(head).astype(BF)
        stack[128:176, here] = jnp.where(iota((48, n), 0) == LEFT, 1.0, tail_t).astype(BF)
        stack[176:280, here] = code.astype(BF)
    summed = mm(stack[...], hot[...])
    counts = summed[WIDTH : WIDTH + 1]
    mean = (summed / jnp.maximum(counts, 1.0)).astype(BF)
    mem = mem_ref[...]
    mem_pad = jnp.concatenate([mem, jnp.zeros((4, SLOTS), F32)], 0)
    state = mem_pad.astype(BF)
    from_in = mm(w_in_ref[...], jnp.concatenate([state, mean], 0)) + b_in_ref[...]
    from_st = mm(w_st_ref[...], state) + b_st_ref[...]
    reset = jax.nn.sigmoid(from_in[0:176] + from_st[0:176])
    update = jax.nn.sigmoid(from_in[176:352] + from_st[176:352])
    candidate = jnp.tanh(from_in[352:528] + reset * from_st[352:528])
    fresh = (1.0 - update) * candidate + update * mem_pad
    new = jnp.where(counts > 0.0, fresh, mem_pad)
    seen = jnp.maximum(counts, seen_ref[...])
    if last:
        flag = jnp.minimum(seen, 1.0)
        outs[0][...] = jnp.where(iota((176, SLOTS), 0) == WIDTH, flag, new)
    else:
        outs[0][...] = new[:WIDTH]
        outs[1][...] = seen


def gru(got, mem_t, seen, weights, last):
    n = OWNERS * PAIR
    if last:
        out = (sds((176, SLOTS), F32),)
    else:
        out = (sds((WIDTH, SLOTS), F32), sds((1, SLOTS), F32))
    return call(
        functools.partial(gru_kernel, last=last),
        out,
        got,
        mem_t,
        seen,
        *weights,
        flops=3e9,
        limit=40 if last else 56,
        scratch_shapes=[pltpu.VMEM((n, SLOTS), BF), pltpu.VMEM((280, n), BF)],
    )


def gru_weights(gru_input, gru_hidden, gru_in_bias, gru_hid_bias, time_freq, time_phase):
    def rows(a, to):
        return jnp.pad(a, [(0, 0), (0, to - a.shape[1])] + [(0, 0)] * (a.ndim - 2))

    w_in = gru_input.T.reshape(3, WIDTH, -1)
    parts = [w_in[:, :, :WIDTH], w_in[:, :, WIDTH : 2 * WIDTH], w_in[:, :, 2 * WIDTH :]]
    parts = [jnp.pad(p, [(0, 0), (0, 4), (0, -p.shape[2] % 8)]) for p in parts]
    w_in = jnp.concatenate(parts, 2).reshape(528, -1)
    w_st = jnp.pad(gru_hidden.T.reshape(3, WIDTH, WIDTH), [(0, 0), (0, 4), (0, 4)]).reshape(528, 176)
    b_in = rows(gru_in_bias.reshape(3, WIDTH), 176).reshape(528, 1)
    b_st = rows(gru_hid_bias.reshape(3, WIDTH), 176).reshape(528, 1)
    freq = jnp.pad(time_freq, (0, 4)).reshape(104, 1)
    phase = jnp.pad(time_phase, (0, 4)).reshape(104, 1)
    return freq, phase, w_in, w_st, b_in, b_st


def slab_exchange(value):
    return lax.all_to_all(value, SLAB, 0, 0, tiled=True)


def zh_all(value):
    copies = jnp.broadcast_to(value[None], (ZH, *value.shape))
    return lax.all_to_all(copies, "zh", 0, 0, tiled=True)


def to_hosts(mem_t):
    zh, y = lax.axis_index("zh"), lax.axis_index("y")
    width = SLOTS // 2
    mine = lax.dynamic_slice_in_dim(mem_t, y // 2 * width, width, 1)
    came = [
        lax.ppermute(
            mine, ("zh", "y"), [(a * ZH + p, (a + p + k) % ZH * ZH + a) for a in range(ZH) for p in range(ZH)]
        )
        for k in (0, 2)
    ]
    straight = (zh - y) % ZH < 2
    low = jnp.where(straight, came[0], came[1])
    high = jnp.where(straight, came[1], came[0])
    return jnp.concatenate([low, high], 1)


def to_homes(sent):
    zh, y = lax.axis_index("zh"), lax.axis_index("y")
    came = [
        lax.ppermute(sent, ("zh", "y"), [(a * ZH + a, a * ZH + (a + k) % ZH) for a in range(ZH)])
        for k in range(1, ZH)
    ]
    return jnp.where(zh == y, sent, sum(came[1:], came[0]))


def body(
    memory,
    node_slot,
    event_nodes,
    event_times,
    valid_mask,
    time_freq,
    time_phase,
    gru_input,
    gru_hidden,
    gru_in_bias,
    gru_hid_bias,
    w_self,
    w_nbr,
    b_embed,
    w_dec1,
    b_dec1,
    w_dec2,
    b_dec2,
):
    zh = jnp.full((1, 1), lax.axis_index("zh"), I32)
    table = node_slot.reshape(512, 128)
    by_column = event_nodes.transpose(0, 2, 1)
    shared = jnp.concatenate([by_column[:, 0:2].reshape(4, EVENTS), event_times, event_times], 0)
    everyone = zh_all(shared)
    ids, times = [], []
    for b in range(2):
        pairs = everyone[:, 2 * b : 2 * b + 2].reshape(8, EVENTS)
        ids.append(jnp.concatenate([pairs, by_column[b, 2:], by_column[b, 2:3]], 0))
        times.append(everyone[:, 4 + b])

    mem_t, _ = lax.optimization_barrier((memory.T, everyone))
    mem_t = to_hosts((mem_t * RANGE).astype(HALF_FLOAT)).astype(F32) * (1.0 / RANGE)
    weights = gru_weights(gru_input, gru_hidden, gru_in_bias, gru_hid_bias, time_freq, time_phase)

    def wide(a, to):
        a = a.reshape(-1, a.shape[-1])
        return jnp.pad(a, [(0, to - a.shape[0]), (0, 128 - a.shape[1])])

    params = jnp.concatenate(
        [
            wide(w_self, 176),
            wide(w_nbr, 176),
            wide(w_dec1[:EMBED], 104),
            wide(w_dec1[EMBED:], 104),
            wide(b_embed, 1),
            wide(b_dec1, 1),
            wide(w_dec2, 1),
            wide(b_dec2, 5),
        ],
        0,
    )

    req0, group0, place0, slot0 = route(ids[0], table)
    req1, group1, place1, slot1 = route(ids[1], table)
    want0 = slab_exchange(req0.reshape(OWNERS, 1, 128)).reshape(OWNERS, 128)
    flat0 = group0[:, :ROWS].reshape(-1, 128)
    flat1 = group1[:, :ROWS].reshape(-1, 128)
    plus = req1 + 32
    riding = jnp.pad(
        jnp.stack([plus >> 5, plus & 31], 1).astype(F32).astype(BF), [(0, 0), (0, 6), (0, 0)]
    )
    rows0 = slab_exchange(gather(want0, mem_t, riding, False))
    came = rows0[:, ROWS + HALF : ROWS + HALF + 2, :].astype(F32)
    want1 = (came[:, 0] * 32.0 + came[:, 1]).astype(I32) - 32

    sent0 = loss_and_letters(rows0, flat0, place0, slot0, times[0], zh, valid_mask[0:1], params, False)[0]
    got0 = slab_exchange(sent0)
    mem_t, seen = gru(got0, mem_t, jnp.zeros((1, SLOTS), F32), weights, False)

    def chunk_total(got):
        part = jnp.sum(got[:, PAIR + CHUNK :, :].astype(F32), 0)
        return jnp.sum(zh_all(part), 0)

    total0 = chunk_total(got0)
    hi = lax.reduce_precision(total0, 8, 7)
    low = (total0 - hi).astype(BF)
    hi = hi.astype(BF)
    rows1 = slab_exchange(gather(want1, mem_t, jnp.concatenate([hi, low], 0), True))
    sent1, params, prev = loss_and_letters(
        rows1, flat1, place1, slot1, times[1], zh, valid_mask[1:2], params, True
    )
    got1 = slab_exchange(sent1)
    total1, last = lax.optimization_barrier((chunk_total(got1), gru(got1, mem_t, seen, weights, True)[0]))
    whole = slab_exchange(jnp.broadcast_to(total1[None], (OWNERS, CHUNK, 128)))
    losses, ws, wn, be, wd, b1, w2, b2 = call(
        final_kernel,
        (
            sds((1, 2), F32),
            sds((WIDTH, EMBED), F32),
            sds((WIDTH, EMBED), F32),
            sds((1, EMBED), F32),
            sds((2 * EMBED, EMBED), F32),
            sds((1, EMBED), F32),
            sds((1, EMBED), F32),
            sds((1, 1), F32),
        ),
        whole,
        params,
        prev,
    )
    final = to_homes((last * RANGE).astype(HALF_FLOAT))
    old, losses = lax.optimization_barrier((memory.T, losses))
    memory_out = jnp.where(final[WIDTH : WIDTH + 1] > 0, final[:WIDTH].astype(F32) * (1.0 / RANGE), old).T
    return (
        memory_out,
        losses.reshape(2),
        ws,
        wn,
        be.reshape(EMBED),
        wd,
        b1.reshape(EMBED),
        w2.reshape(EMBED),
        b2.reshape(1),
    )


def solution(mesh):
    finer = Mesh(mesh.devices.reshape(4, ZH, 2, 2, ZH), ALL)
    return jax.shard_map(
        body,
        mesh=finer,
        in_specs=(P(HOME, None), P(), P(None, ALL, None), P(None, ALL), P(None, ALL)) + (P(),) * 13,
        out_specs=(P(HOME, None),) + (P(),) * 8,
        check_vma=False,
    )
```

```python
import functools

import jax
import jax.numpy as jnp
from jax import lax
from jax.experimental import pallas as pl
from jax.experimental.pallas import tpu as pltpu
from jax.sharding import Mesh
from jax.sharding import PartitionSpec as P

HOME = ("x", "zh", "zl", "c")
SLAB = ("x", "y", "zl", "c")
ALL = ("x", "zh", "zl", "c", "y")
ZH = 4
OWNERS = 64
EVENTS = 128
WIDTH = 172
EMBED = 100
SLOTS = 1024
PAIR = 8 * ZH
ROWS = 112
HALF = 56
LEFT = WIDTH - 128
POSITIONS = OWNERS * ROWS
CHUNK = 16
STEP_DEV = 16
STEP = 4.0
F32 = jnp.float32
BF = jnp.bfloat16
HALF_FLOAT = jnp.float16
RANGE = 8192.0
I32 = jnp.int32
AT_NBR, AT_DEC_A, AT_DEC_B, AT_VEC = 176, 352, 456, 560
PARAM_ROWS = 568
GRAD_ROWS = OWNERS * CHUNK


def iota(shape, dim):
    return lax.broadcasted_iota(I32, shape, dim)


def mm(a, b):
    return jnp.dot(a, b, preferred_element_type=F32)


def mm_nt(a, b):
    return lax.dot_general(a, b, (((1,), (1,)), ((), ())), preferred_element_type=F32)


def call(kernel, out_shape, *args, flops=1e8, limit=56, **kw):
    moved = sum(a.size * a.dtype.itemsize for a in args)
    return pl.pallas_call(
        kernel,
        out_shape=out_shape,
        compiler_params=pltpu.CompilerParams(vmem_limit_bytes=limit << 20),
        cost_estimate=pl.CostEstimate(flops=int(flops), bytes_accessed=int(moved), transcendentals=0),
        **kw,
    )(*args)


def sds(shape, dtype):
    return jax.ShapeDtypeStruct(shape, dtype)


def route_kernel(ids_ref, table_ref, req_ref, group_ref, place_ref, slot_ref, table_t):
    t = table_ref[...]
    table_t[0:128, :] = jnp.transpose((t >> 8).astype(F32)).astype(BF)
    table_t[128:256, :] = jnp.transpose((t & 255).astype(F32)).astype(BF)
    upper = (iota((128, 128), 0) < iota((128, 128), 1)).astype(F32)
    both = jnp.concatenate([upper, jnp.ones((128, 128), F32)], 1).astype(BF)
    lane = iota((1, 128), 1)
    acc = jnp.zeros((4 * OWNERS, 128), F32)
    base = jnp.zeros((OWNERS, 128), F32)
    for part in range(5):
        ids = [ids_ref[part * 8 + r : part * 8 + r + 1, :] for r in range(8)]
        rows = 7 if part == 4 else 8
        hot = jnp.concatenate(
            [(iota((512, 128), 0) == (n >> 7)).astype(F32).astype(BF) for n in ids[:rows]], 1
        )
        picked = mm(table_t[...], hot)
        sent = []
        slots = []
        for r in range(rows):
            low = iota((128, 128), 0) == (ids[r] & 127)
            hi = jnp.sum(jnp.where(low, picked[:128, r * 128 : (r + 1) * 128], 0.0), 0, keepdims=True)
            lo = jnp.sum(jnp.where(low, picked[128:, r * 128 : (r + 1) * 128], 0.0), 0, keepdims=True)
            slot = (hi * 256.0 + lo).astype(I32)
            slots.append(slot & (SLOTS - 1))
            sent.append(slot >> 10)
        own = [iota((OWNERS, 128), 0) == d for d in sent]
        own_f = [o.astype(F32) for o in own]
        counted = mm(jnp.concatenate([o.astype(BF) for o in own_f], 0), both)
        for r in range(rows):
            mine = counted[r * OWNERS : (r + 1) * OWNERS]
            if part == 0 and r % 2 == 0:
                base = jnp.zeros((OWNERS, 128), F32)
            if part == 1 and r == 0:
                base = jnp.zeros((OWNERS, 128), F32)
            rank = jnp.sum(own_f[r] * (mine[:, :128] + base), 0, keepdims=True).astype(I32)
            base = base + mine[:, 128:]
            plus = slots[r] + 1
            if part == 0:
                where = (r // 2) * 8 + rank
                place_ref[r : r + 1, :] = sent[r] * 8 + rank
                slot_ref[r : r + 1, :] = plus
                ghi = glo = jnp.zeros((1, 128), F32)
            else:
                where = PAIR + rank
                row = (part - 1) * 8 + r
                kind = 3 if row == 0 else (row - 1) // 10
                ghi = jnp.full((1, 128), float(kind + 1), F32)
                glo = lane.astype(F32)
            at = (iota((128, 128), 0) == where).astype(F32).astype(BF)
            planes = [(slots[r] >> 5).astype(F32) + 1.0, (slots[r] & 31).astype(F32), ghi, glo]
            left = jnp.concatenate([own_f[r] * v for v in planes], 0).astype(BF)
            acc = acc + mm_nt(left, at)
    o = OWNERS
    req_ref[...] = ((acc[0:o] - 1.0) * 32.0 + acc[o : 2 * o]).astype(I32)
    group_ref[...] = ((acc[2 * o : 3 * o] - 1.0) * 128.0 + acc[3 * o :]).astype(I32)


def route(ids, table):
    return call(
        route_kernel,
        (sds((OWNERS, 128), I32), sds((OWNERS, 128), I32), sds((8, 128), I32), sds((8, 128), I32)),
        ids,
        table,
        flops=3e9,
        scratch_shapes=[pltpu.VMEM((256, 512), BF)],
    )


def gather_kernel(want_ref, mem_ref, extra_ref, out_ref, mem_rows, *, shared):
    @pl.when(pl.program_id(0) == 0)
    def _():
        m = jnp.concatenate([mem_ref[...], jnp.zeros((4, SLOTS), F32)], 0)
        mem_rows[:, 0:128] = jnp.transpose(m[0:128]).astype(BF)
        tail = jnp.concatenate([m[128:], jnp.zeros((80, SLOTS), F32)], 0)
        mem_rows[:, 128:256] = jnp.transpose(tail).astype(BF)

    cols = jnp.transpose(want_ref[...].astype(F32)).astype(I32)
    lane = iota((ROWS, SLOTS), 1).astype(jnp.int16)

    def hot_of(j):
        col = jnp.broadcast_to(cols[0:ROWS, j : j + 1], (ROWS, 128)).astype(jnp.int16)
        return jnp.where(lane == jnp.concatenate([col] * (SLOTS // 128), 1), BF(1), BF(0))

    rows = mm(jnp.concatenate([hot_of(j) for j in range(STEP_DEV)], 0), mem_rows[...])
    for j in range(STEP_DEV):
        mine = rows[j * ROWS : (j + 1) * ROWS]
        tail = mine[:HALF, 128:] + pltpu.roll(mine[HALF:, 128:], 64, 1)
        extra = extra_ref[...] if shared else extra_ref[j]
        out_ref[j, 0:ROWS, :] = mine[:, :128].astype(BF)
        out_ref[j, ROWS : ROWS + HALF, :] = tail.astype(BF)
        out_ref[j, ROWS + HALF :, :] = extra


def gather(want, mem_t, extra, shared):
    more = extra.shape[-2]
    total = ROWS + HALF + more
    if shared:
        extra_spec = pl.BlockSpec((more, 128), lambda i: (0, 0))
    else:
        extra_spec = pl.BlockSpec((STEP_DEV, more, 128), lambda i: (i, 0, 0))
    return call(
        functools.partial(gather_kernel, shared=shared),
        sds((OWNERS, total, 128), BF),
        want,
        mem_t,
        extra,
        flops=4e9,
        limit=28,
        grid=(OWNERS // STEP_DEV,),
        in_specs=[
            pl.BlockSpec((STEP_DEV, 128), lambda i: (i, 0)),
            pl.BlockSpec((WIDTH, SLOTS), lambda i: (0, 0)),
            extra_spec,
        ],
        out_specs=pl.BlockSpec((STEP_DEV, total, 128), lambda i: (i, 0, 0)),
        scratch_shapes=[pltpu.VMEM((SLOTS, 256), BF)],
    )


def stepped(params, grads):
    row, col = iota((PARAM_ROWS, 128), 0), iota((PARAM_ROWS, 128), 1)
    real = (row < AT_VEC + 3) | ((row == AT_VEC + 3) & (col == 0))
    grads = jnp.where(real, grads, 0.0)
    norm = jnp.sqrt(jnp.sum(grads * grads))
    return params - (STEP / (norm + 1e-06)) * grads


def vectors_of(grads):
    return grads[AT_VEC : AT_VEC + 8] + grads[AT_VEC + 8 : AT_VEC + 16] + grads[AT_VEC + 16 : AT_VEC + 24]


def joined(flat):
    return jnp.concatenate([flat[:AT_VEC], vectors_of(flat)], 0)


def softplus(x):
    return jnp.maximum(x, 0.0) + jnp.log1p(jnp.exp(-jnp.abs(x)))


def loss_kernel(*refs, update):
    (rows_ref, group_ref, place_ref, slot_ref, time_ref, zh_ref, valid_ref, param_ref), outs = refs[:8], refs[8:]
    if update:
        out_ref, param_out_ref, prev_ref, rows256, select = outs
        got = rows_ref[:, ROWS + HALF :, :].astype(F32)
        flat = (got[:, :CHUNK] + got[:, CHUNK:]).reshape(GRAD_ROWS, 128)
        grads = joined(flat)
        params = stepped(param_ref[...], grads)
        param_out_ref[...] = params
        prev_ref[...] = grads[AT_VEC:]
    else:
        out_ref, rows256, select = outs
        params = param_ref[...]

    rows256[:, :, 0:128] = rows_ref[:, 0:ROWS, :]
    tails = rows_ref[:, ROWS : ROWS + HALF, :]
    rows256[:, 0:HALF, 128:256] = tails
    rows256[:, HALF:ROWS, 128:256] = pltpu.roll(tails.astype(F32), 64, 2).astype(BF)

    codes = iota((512, 128), 0).astype(jnp.int16)
    for t in range(POSITIONS // 128):
        wanted = jnp.broadcast_to(group_ref[t : t + 1, :], (512, 128)).astype(jnp.int16)
        select[:, t * 128 : (t + 1) * 128] = jnp.where(codes == wanted, BF(1), BF(0))
    summed = mm(select[...], rows256[...].reshape(POSITIONS, 256))
    nbr = summed[: 3 * EVENTS]

    lane256 = iota((EVENTS, 256), 1)
    place = place_ref[...]
    place_c = jnp.transpose(place.astype(F32)).astype(I32)
    plus = slot_ref[...]
    time = time_ref[...]
    info = jnp.concatenate(
        [(plus >> 5).astype(F32), (plus & 31).astype(F32), (time >> 5).astype(F32), (time & 31).astype(F32)], 0
    )
    info_c = jnp.transpose(info)

    tails_out = []
    own = []
    for d in range(ZH):
        held = rows256[:, d * 8 : (d + 1) * 8, :].reshape(OWNERS * 8, 256)
        picked = []
        spread = []
        marked = []
        for c in range(2):
            r = 2 * d + c
            take = (iota((EVENTS, OWNERS * 8), 1) == place_c[:, r : r + 1]).astype(F32).astype(BF)
            x = mm(take, held)
            picked.append(jnp.where(lane256 < WIDTH, x, 0.0))
            spread.append((iota((OWNERS * 8, EVENTS), 0) == place[r : r + 1, :]).astype(F32).astype(BF))
            marks = jnp.zeros((EVENTS, 256), F32)
            for k, col in enumerate((r, 8 + r, 16 + d, 20 + d)):
                marks = jnp.where(lane256 == WIDTH + k, info_c[:, col : col + 1], marks)
            marked.append(marks)
        to_first = (picked[1] + marked[0]).astype(BF)
        to_second = (picked[0] + marked[1]).astype(BF)
        letters = mm(spread[0], to_first) + mm(spread[1], to_second)
        out_ref[:, d * 8 : (d + 1) * 8, :] = letters[:, :128].reshape(OWNERS, 8, 128).astype(BF)
        tails_out.append(letters[:, 128:])
        mine = (zh_ref[...] == d).astype(F32)
        own = [p * mine if d == 0 else o + p * mine for p, o in zip(picked, own or picked)]
    for d in range(2):
        tail = tails_out[d] + pltpu.roll(tails_out[d + 2], 64, 1)
        out_ref[:, PAIR + d * 8 : PAIR + (d + 1) * 8, :] = tail.reshape(OWNERS, 8, 128).astype(BF)

    own_rows = jnp.concatenate(own + [jnp.where(lane256 < WIDTH, summed[3 * EVENTS :], 0.0)], 0).astype(BF)
    zeros = jnp.zeros((80, 128), F32)
    w_self = jnp.concatenate([params[0:AT_NBR], zeros], 0).astype(BF)
    w_nbr = jnp.concatenate([params[AT_NBR:AT_DEC_A], zeros], 0).astype(BF)
    pad = jnp.zeros((24, 128), F32)
    dec_a = jnp.concatenate([params[AT_DEC_A:AT_DEC_B], pad], 0).astype(BF)
    dec_b = jnp.concatenate([params[AT_DEC_B:AT_VEC], pad], 0).astype(BF)
    b_embed = params[AT_VEC : AT_VEC + 1]
    b_dec1 = params[AT_VEC + 1 : AT_VEC + 2]
    w_dec2 = params[AT_VEC + 2 : AT_VEC + 3]
    b_dec2 = params[AT_VEC + 3 : AT_VEC + 4, 0:1]
    nbr_hi = nbr.astype(BF)
    nbr_lo = (nbr - nbr_hi.astype(F32)).astype(BF)
    mean = (mm(nbr_hi, w_nbr) + mm(nbr_lo, w_nbr)) * 0.1
    act = jnp.tanh(mm(own_rows, w_self) + mean + b_embed)
    hidden = act.astype(BF)
    first = jnp.concatenate([hidden[:EVENTS], hidden[:EVENTS]], 0)
    second = hidden[EVENTS:]
    pre = mm(first, dec_a) + mm(second, dec_b) + b_dec1
    inner = jnp.maximum(pre, 0.0)
    logits = jnp.sum(inner * w_dec2, 1, keepdims=True) + b_dec2
    valid_row = valid_ref[...].astype(F32)
    valid = jnp.transpose(jnp.broadcast_to(valid_row, (128, 128)))[:, 0:1]
    valid = jnp.concatenate([valid, valid], 0)
    sign = jnp.where(iota((2 * EVENTS, 1), 0) < EVENTS, -1.0, 1.0)
    loss = jnp.sum(softplus(sign * logits) * valid)
    count = jnp.sum(valid_row)
    d_logit = sign * jax.nn.sigmoid(sign * logits) * valid
    d_inner = jnp.where(pre > 0.0, d_logit * w_dec2, 0.0)
    d_bf = d_inner.astype(BF)
    g_dec2 = jnp.sum(inner * d_logit, 0, keepdims=True)
    g_b2 = jnp.sum(d_logit)
    g_b1 = jnp.sum(d_inner, 0, keepdims=True)
    d_first = mm_nt(d_bf, dec_a).astype(BF).astype(F32)
    d_second = mm_nt(d_bf, dec_b).astype(BF).astype(F32)
    d_zero = (d_first[:EVENTS] + d_first[EVENTS:]).astype(BF).astype(F32)
    d_pre = jnp.concatenate([d_zero, d_second], 0) * (1.0 - act * act)
    g_be = jnp.sum(d_pre, 0, keepdims=True)

    def mm_tn(a, b):
        return mm(jnp.transpose(a.astype(F32)).astype(BF), b)

    g_self = mm_tn(own_rows, d_pre.astype(BF))[:176]
    d_mean = (d_pre * 0.1).astype(BF)
    g_nbr = (mm_tn(nbr_hi, d_mean) + mm_tn(nbr_lo, d_mean))[:176]
    g_nbr = jnp.where(iota((176, 128), 0) < WIDTH, g_nbr, 0.0)
    g_a = mm_tn(first, d_bf)[:104]
    g_b = mm_tn(second, d_bf)[:104]
    one = jnp.ones((1, 128), F32)
    vec = jnp.concatenate([g_be, g_b1, g_dec2, g_b2 * one, loss * one, count * one, one * 0.0, one * 0.0], 0)
    hi = vec.astype(BF).astype(F32)
    mid = (vec - hi).astype(BF).astype(F32)
    low = vec - hi - mid
    rest = jnp.zeros((GRAD_ROWS - AT_VEC - 24, 128), F32)
    grads = jnp.concatenate([g_self, g_nbr, g_a, g_b, hi, mid, low, rest], 0)
    out_ref[:, PAIR + CHUNK :, :] = grads.reshape(OWNERS, CHUNK, 128).astype(BF)


def loss_and_letters(rows, group, place, slot, time, zh, valid, params, update):
    out = [sds((OWNERS, PAIR + CHUNK + CHUNK, 128), BF)]
    if update:
        out += [sds((PARAM_ROWS, 128), F32), sds((8, 128), F32)]
    return call(
        functools.partial(loss_kernel, update=update),
        tuple(out),
        rows,
        group,
        place,
        slot,
        time,
        zh,
        valid,
        params,
        flops=1e10,
        limit=40,
        scratch_shapes=[pltpu.VMEM((OWNERS, ROWS, 256), BF), pltpu.VMEM((512, POSITIONS), BF)],
    )


def final_kernel(got_ref, param_ref, prev_ref, loss_ref, ws_ref, wn_ref, be_ref, wd_ref, b1_ref, w2_ref, b2_ref):
    grads = joined(got_ref[...].reshape(GRAD_ROWS, 128))
    params = stepped(param_ref[...], grads)
    vec = grads[AT_VEC:]
    prev = prev_ref[...]
    first = prev[4:5] / jnp.maximum(prev[5:6], 1.0)
    second = vec[4:5] / jnp.maximum(vec[5:6], 1.0)
    loss_ref[...] = jnp.where(iota((1, 128), 1) == 0, first, second)[:, 0:2]
    ws_ref[...] = params[0:WIDTH, :EMBED]
    wn_ref[...] = params[AT_NBR : AT_NBR + WIDTH, :EMBED]
    wd_ref[0:EMBED, :] = params[AT_DEC_A : AT_DEC_A + EMBED, :EMBED]
    wd_ref[EMBED:, :] = params[AT_DEC_B : AT_DEC_B + EMBED, :EMBED]
    be_ref[...] = params[AT_VEC : AT_VEC + 1, :EMBED]
    b1_ref[...] = params[AT_VEC + 1 : AT_VEC + 2, :EMBED]
    w2_ref[...] = params[AT_VEC + 2 : AT_VEC + 3, :EMBED]
    b2_ref[...] = params[AT_VEC + 3 : AT_VEC + 4, 0:1]


def gru_kernel(
    got_ref, mem_ref, seen_ref, freq_ref, phase_ref, w_in_ref, w_st_ref, b_in_ref, b_st_ref, *outs, last
):
    hot, stack = outs[-2:]
    half = PAIR // 2
    for h in range(2):
        n = OWNERS * half
        head = got_ref[:, h * half : (h + 1) * half, :].reshape(n, 128).astype(F32)
        tail = got_ref[:, PAIR : PAIR + half, :].reshape(n, 128).astype(F32)
        if h:
            tail = pltpu.roll(tail, 64, 1)
        col = (tail[:, LEFT : LEFT + 1] * 32.0 + tail[:, LEFT + 1 : LEFT + 2]).astype(I32) - 1
        col = jnp.broadcast_to(col, (n, 128)).astype(jnp.int16)
        slots = iota((n, SLOTS), 1).astype(jnp.int16)
        hot[h * n : (h + 1) * n, :] = jnp.where(slots == jnp.concatenate([col] * (SLOTS // 128), 1), BF(1), BF(0))
        here = pl.ds(h * n, n)
        tail_t = jnp.transpose(tail)[0:48]
        when = tail_t[46:47] * 32.0 + tail_t[47:48]
        code = jnp.cos(freq_ref[...] * when + phase_ref[...])
        stack[0:128, here] = jnp.transpose(head).astype(BF)
        stack[128:176, here] = jnp.where(iota((48, n), 0) == LEFT, 1.0, tail_t).astype(BF)
        stack[176:280, here] = code.astype(BF)
    summed = mm(stack[...], hot[...])
    counts = summed[WIDTH : WIDTH + 1]
    mean = (summed / jnp.maximum(counts, 1.0)).astype(BF)
    mem = mem_ref[...]
    mem_pad = jnp.concatenate([mem, jnp.zeros((4, SLOTS), F32)], 0)
    state = mem_pad.astype(BF)
    from_in = mm(w_in_ref[...], jnp.concatenate([state, mean], 0)) + b_in_ref[...]
    from_st = mm(w_st_ref[...], state) + b_st_ref[...]
    reset = jax.nn.sigmoid(from_in[0:176] + from_st[0:176])
    update = jax.nn.sigmoid(from_in[176:352] + from_st[176:352])
    candidate = jnp.tanh(from_in[352:528] + reset * from_st[352:528])
    fresh = (1.0 - update) * candidate + update * mem_pad
    new = jnp.where(counts > 0.0, fresh, mem_pad)
    seen = jnp.maximum(counts, seen_ref[...])
    if last:
        flag = jnp.minimum(seen, 1.0)
        outs[0][...] = jnp.where(iota((176, SLOTS), 0) == WIDTH, flag, new)
    else:
        outs[0][...] = new[:WIDTH]
        outs[1][...] = seen


def gru(got, mem_t, seen, weights, last):
    n = OWNERS * PAIR
    if last:
        out = (sds((176, SLOTS), F32),)
    else:
        out = (sds((WIDTH, SLOTS), F32), sds((1, SLOTS), F32))
    return call(
        functools.partial(gru_kernel, last=last),
        out,
        got,
        mem_t,
        seen,
        *weights,
        flops=3e9,
        limit=40 if last else 56,
        scratch_shapes=[pltpu.VMEM((n, SLOTS), BF), pltpu.VMEM((280, n), BF)],
    )


def gru_weights(gru_input, gru_hidden, gru_in_bias, gru_hid_bias, time_freq, time_phase):
    def rows(a, to):
        return jnp.pad(a, [(0, 0), (0, to - a.shape[1])] + [(0, 0)] * (a.ndim - 2))

    w_in = gru_input.T.reshape(3, WIDTH, -1)
    parts = [w_in[:, :, :WIDTH], w_in[:, :, WIDTH : 2 * WIDTH], w_in[:, :, 2 * WIDTH :]]
    parts = [jnp.pad(p, [(0, 0), (0, 4), (0, -p.shape[2] % 8)]) for p in parts]
    w_in = jnp.concatenate(parts, 2).reshape(528, -1)
    w_st = jnp.pad(gru_hidden.T.reshape(3, WIDTH, WIDTH), [(0, 0), (0, 4), (0, 4)]).reshape(528, 176)
    b_in = rows(gru_in_bias.reshape(3, WIDTH), 176).reshape(528, 1)
    b_st = rows(gru_hid_bias.reshape(3, WIDTH), 176).reshape(528, 1)
    freq = jnp.pad(time_freq, (0, 4)).reshape(104, 1)
    phase = jnp.pad(time_phase, (0, 4)).reshape(104, 1)
    return freq, phase, w_in, w_st, b_in, b_st


def slab_exchange(value):
    return lax.all_to_all(value, SLAB, 0, 0, tiled=True)


def zh_all(value):
    copies = jnp.broadcast_to(value[None], (ZH, *value.shape))
    return lax.all_to_all(copies, "zh", 0, 0, tiled=True)


def to_hosts(mem_t):
    zh, y = lax.axis_index("zh"), lax.axis_index("y")
    width = SLOTS // 2
    mine = lax.dynamic_slice_in_dim(mem_t, y // 2 * width, width, 1)
    came = [
        lax.ppermute(
            mine, ("zh", "y"), [(a * ZH + p, (a + p + k) % ZH * ZH + a) for a in range(ZH) for p in range(ZH)]
        )
        for k in (0, 2)
    ]
    straight = (zh - y) % ZH < 2
    low = jnp.where(straight, came[0], came[1])
    high = jnp.where(straight, came[1], came[0])
    return jnp.concatenate([low, high], 1)


def to_homes(sent):
    zh, y = lax.axis_index("zh"), lax.axis_index("y")
    came = [
        lax.ppermute(sent, ("zh", "y"), [(a * ZH + a, a * ZH + (a + k) % ZH) for a in range(ZH)])
        for k in range(1, ZH)
    ]
    return jnp.where(zh == y, sent, sum(came[1:], came[0]))


def body(
    memory,
    node_slot,
    event_nodes,
    event_times,
    valid_mask,
    time_freq,
    time_phase,
    gru_input,
    gru_hidden,
    gru_in_bias,
    gru_hid_bias,
    w_self,
    w_nbr,
    b_embed,
    w_dec1,
    b_dec1,
    w_dec2,
    b_dec2,
):
    zh = jnp.full((1, 1), lax.axis_index("zh"), I32)
    table = node_slot.reshape(512, 128)
    by_column = event_nodes.transpose(0, 2, 1)
    shared = jnp.concatenate([by_column[:, 0:2].reshape(4, EVENTS), event_times, event_times], 0)
    everyone = zh_all(shared)
    ids, times = [], []
    for b in range(2):
        pairs = everyone[:, 2 * b : 2 * b + 2].reshape(8, EVENTS)
        ids.append(jnp.concatenate([pairs, by_column[b, 2:], by_column[b, 2:3]], 0))
        times.append(everyone[:, 4 + b])

    mem_t, _ = lax.optimization_barrier((memory.T, everyone))
    mem_t = to_hosts((mem_t * RANGE).astype(HALF_FLOAT)).astype(F32) * (1.0 / RANGE)
    weights = gru_weights(gru_input, gru_hidden, gru_in_bias, gru_hid_bias, time_freq, time_phase)

    def wide(a, to):
        a = a.reshape(-1, a.shape[-1])
        return jnp.pad(a, [(0, to - a.shape[0]), (0, 128 - a.shape[1])])

    params = jnp.concatenate(
        [
            wide(w_self, 176),
            wide(w_nbr, 176),
            wide(w_dec1[:EMBED], 104),
            wide(w_dec1[EMBED:], 104),
            wide(b_embed, 1),
            wide(b_dec1, 1),
            wide(w_dec2, 1),
            wide(b_dec2, 5),
        ],
        0,
    )

    req0, group0, place0, slot0 = route(ids[0], table)
    req1, group1, place1, slot1 = route(ids[1], table)
    want0 = slab_exchange(req0.reshape(OWNERS, 1, 128)).reshape(OWNERS, 128)
    flat0 = group0[:, :ROWS].reshape(-1, 128)
    flat1 = group1[:, :ROWS].reshape(-1, 128)
    plus = req1 + 32
    riding = jnp.pad(
        jnp.stack([plus >> 5, plus & 31], 1).astype(F32).astype(BF), [(0, 0), (0, 6), (0, 0)]
    )
    rows0 = slab_exchange(gather(want0, mem_t, riding, False))
    came = rows0[:, ROWS + HALF : ROWS + HALF + 2, :].astype(F32)
    want1 = (came[:, 0] * 32.0 + came[:, 1]).astype(I32) - 32

    sent0 = loss_and_letters(rows0, flat0, place0, slot0, times[0], zh, valid_mask[0:1], params, False)[0]
    got0 = slab_exchange(sent0)
    mem_t, seen = gru(got0, mem_t, jnp.zeros((1, SLOTS), F32), weights, False)

    def chunk_total(got):
        part = jnp.sum(got[:, PAIR + CHUNK :, :].astype(F32), 0)
        return jnp.sum(zh_all(part), 0)

    total0 = chunk_total(got0)
    hi = lax.reduce_precision(total0, 8, 7)
    low = (total0 - hi).astype(BF)
    hi = hi.astype(BF)
    rows1 = slab_exchange(gather(want1, mem_t, jnp.concatenate([hi, low], 0), True))
    sent1, params, prev = loss_and_letters(
        rows1, flat1, place1, slot1, times[1], zh, valid_mask[1:2], params, True
    )
    got1 = slab_exchange(sent1)
    last = (gru(got1, mem_t, seen, weights, True)[0] * RANGE).astype(HALF_FLOAT)
    total1, last = lax.optimization_barrier((chunk_total(got1), last))
    whole = slab_exchange(jnp.broadcast_to(total1[None], (OWNERS, CHUNK, 128)))
    losses, ws, wn, be, wd, b1, w2, b2 = call(
        final_kernel,
        (
            sds((1, 2), F32),
            sds((WIDTH, EMBED), F32),
            sds((WIDTH, EMBED), F32),
            sds((1, EMBED), F32),
            sds((2 * EMBED, EMBED), F32),
            sds((1, EMBED), F32),
            sds((1, EMBED), F32),
            sds((1, 1), F32),
        ),
        whole,
        params,
        prev,
    )
    final = to_homes(last)
    memory_out = jnp.where(final[WIDTH : WIDTH + 1] > 0, final[:WIDTH].astype(F32) * (1.0 / RANGE), memory.T).T
    return (
        memory_out,
        losses.reshape(2),
        ws,
        wn,
        be.reshape(EMBED),
        wd,
        b1.reshape(EMBED),
        w2.reshape(EMBED),
        b2.reshape(1),
    )


def solution(mesh):
    finer = Mesh(mesh.devices.reshape(4, ZH, 2, 2, ZH), ALL)
    return jax.shard_map(
        body,
        mesh=finer,
        in_specs=(P(HOME, None), P(), P(None, ALL, None), P(None, ALL), P(None, ALL)) + (P(),) * 13,
        out_specs=(P(HOME, None),) + (P(),) * 8,
        check_vma=False,
    )
```
